32 devices in a mesh: az: 4 (over z), rad: 2 (over x), ax: 4 (over y, core).
Axes of the slice: x: 2, y: 2, z: 4, core: 2. Of those that a mesh axis runs over, the one named last changes fastest.
Arguments:
- cycle: float32 [4, 5, 512, 4096], P(None, None, ('rad', 'ax'), 'az'), may hold values from -6 to 6
- field: float32 [5, 64, 8, 4096], P(None, 'rad', 'ax', 'az'), may hold values from -6 to 6
- shift: int32 [1], replicated, may hold values from 0 to 4095
- owner: int32 [64, 8], P('rad', 'ax'), may hold values 0 or 1
Outputs:
- field_next: float32 [5, 64, 8, 4096], P(None, 'rad', 'ax', 'az')
- shifted_cycle: float32 [4, 5, 512, 4096], P(None, None, ('rad', 'ax'), 'az')
The draws below stay inside these ranges and needn't reach their ends.
All inputs are finite; a program needn't handle non-finite values. No bound on the sum of `owner` on one device may be relied on, other than what follows from the above.
Results may differ from the reference program's by a relative error of at most 0.00007.
Values sent between devices are 32-bit elements; how exact they have to be, the bound alone decides.
A program may use at most 192 MiB of HBM per device.

```python
import math
import jax
import jax.numpy as jnp
from jax import lax

NTH = 4096
LAY = 4
VARS = 5
KR = 8
NR = 512
NRS = 64
NZS = 8


def plant(values, own_key, low, largest):
    spot = [jax.random.randint(jax.random.fold_in(own_key, axis), (), 0, length) for axis, length in enumerate(values.shape)]
    widest = values.shape.index(max(values.shape))
    next_to = spot[:widest] + [(spot[widest] + 1) % values.shape[widest]] + spot[widest + 1:]
    return values.at[tuple(spot)].set(low).at[tuple(next_to)].set(largest)


def block_levels(stream_key, shape, cuts, least, top_value):
    def one(dim, shards_of):
        draws = jax.random.uniform(jax.random.fold_in(jax.random.fold_in(stream_key, 6), dim), (shards_of,), jnp.float32, least / len(cuts), top_value / len(cuts))
        return jnp.repeat(jnp.exp(draws), shape[dim] // shards_of).reshape((-1,) + (1,) * (len(shape) - dim - 1))

    level = one(*cuts[0])
    for cut in cuts[1:]:
        level = level * one(*cut)
    return level


def centred(stream_key, extent, scale, bound, pieces=(), kind=jnp.bfloat16):
    drawn = scale * jax.random.normal(stream_key, extent, jnp.float32)
    if pieces:
        drawn = drawn * block_levels(stream_key, extent, pieces, -0.22, 0.18)
    return jnp.clip(drawn, -bound, bound).astype(kind)


def setup_inputs(seed: int = 0) -> dict:
    seeds = jax.random.split(jax.random.key(seed), 5)
    return {
        "cycle": centred(seeds[0], (LAY, VARS, NR, NTH), 1.0, 6.0, ((2, 8), (3, 4)), jnp.float32),
        "field": centred(seeds[1], (VARS, NRS, NZS, NTH), 1.0, 6.0, ((1, 2), (2, 4), (3, 4)), jnp.float32),
        "shift": jax.random.randint(seeds[2], (1,), 0, NTH).astype(jnp.int32),
        "owner": plant((jax.random.randint(seeds[3], (NRS, NZS), 0, 4) < 3).astype(jnp.int32), jax.random.fold_in(seeds[3], 1), 0, 1),
    }


LAYER_WEIGHTS = (0.4, 0.3, 0.2, 0.1)
AXIAL_SPEEDS = (0.35, 0.2, 0.3, 0.25, 0.4)
DIFFUSION = 0.15
SWIRL_SPEED = 0.1


def shift_layer(layer, shift):
    spectrum = jnp.fft.fft(layer, axis=-1)
    wave = jnp.arange(NTH, dtype=jnp.int32)
    folded = jnp.minimum(wave, NTH - wave)
    filt = (3 * folded < NTH).astype(jnp.float32)
    phase = jnp.remainder(wave * shift[0], NTH).astype(jnp.float32) * (2.0 * math.pi / NTH)
    gain = filt * jnp.exp(-1j * phase)
    return jnp.real(jnp.fft.ifft(spectrum * gain, axis=-1)).astype(jnp.float32)


def reference(cycle, field, shift, owner):
    shifted_cycle = lax.map(lambda layer: shift_layer(layer, shift), cycle)
    weights = jnp.array(LAYER_WEIGHTS, jnp.float32)
    grouped = shifted_cycle.reshape(LAY, VARS, NRS, KR, NTH)
    ghost = jnp.einsum('l,lvrkt->vrt', weights, grouped, precision=lax.Precision.HIGHEST) / KR
    mask = owner.astype(jnp.float32)[:, :, None]
    speeds = jnp.array(AXIAL_SPEEDS, jnp.float32)

    def advance(inputs):
        state0, ghost_var, speed = inputs

        def rates(state):
            radial_pad = jnp.pad(state, ((1, 1), (0, 0), (0, 0)))
            zeros_top = jnp.zeros_like(state[:, :1])
            axial_pad = jnp.concatenate([ghost_var[:, None], state, zeros_top], axis=1)
            outward = radial_pad[2:]
            inward = radial_pad[:-2]
            above = axial_pad[:, 2:]
            below = axial_pad[:, :-2]
            return mask * (DIFFUSION * (outward + inward + above + below - 4.0 * state)
                           - 0.5 * speed * (above - below) - 0.5 * SWIRL_SPEED * (outward - inward))

        first = rates(state0)
        second = rates(state0 + 0.5 * first)
        third = rates(state0 + 0.5 * second)
        fourth = rates(state0 + third)
        return state0 + (first + 2.0 * second + 2.0 * third + fourth) / 6.0

    field_next = lax.map(advance, (field, ghost, speeds))
    return field_next, shifted_cycle
```

```python
import math

import jax
import jax.numpy as jnp
import numpy as np
from jax import lax
from jax.experimental import pallas as pl
from jax.experimental.pallas import tpu as pltpu
from jax.sharding import PartitionSpec as P

KR = 8


LAYER_WEIGHTS = (0.4, 0.3, 0.2, 0.1)
AXIAL_SPEEDS = (0.35, 0.2, 0.3, 0.25, 0.4)
DIFFUSION = 0.15
SWIRL_SPEED = 0.1
MIB = 1024 * 1024


def class_counts(length):
    top = (length - 1) // 3
    kept = np.arange(-top, top + 1)
    first = kept[kept % 4 == 1]
    assert length % 4 == 0 and (first - 1).sum() == 0
    even, odd, half = [int((kept % 4 == r).sum()) for r in (0, 1, 2)]
    assert even == odd
    return even, half


def shift_tables(shift_value, length):
    quarter = length // 4
    even, half = class_counts(length)
    target = jnp.arange(quarter, dtype=jnp.int32) - shift_value
    rows = []
    for count in (even, half):
        angle = jnp.remainder(count * target, 2 * quarter).astype(jnp.float32) * (math.pi / quarter)
        rows += [jnp.sin(angle), jnp.cos(angle)]
    angle = jnp.remainder(target, length).astype(jnp.float32) * (2.0 * math.pi / length)
    rows += [jnp.cos(angle), jnp.sin(angle)]
    source = np.arange(quarter) * (2.0 * np.pi / length)
    rows += [jnp.asarray(np.cos(source), jnp.float32), jnp.asarray(np.sin(source), jnp.float32)]
    return jnp.stack(rows)


def source_tables(length):
    quarter = length // 4
    source = np.arange(quarter)
    cols = []
    for count in class_counts(length):
        angle = (count * source % (2 * quarter)) * (np.pi / quarter)
        cols += [np.sin(angle), np.cos(angle)]
    return jnp.asarray(np.stack(cols, axis=1), jnp.float32)


def kernel_matrix_body(length, block, shift_ref, rows_ref, cols_ref, eh_ref, el_ref, hh_ref, hl_ref):
    quarter = length // 4
    even, half = class_counts(length)
    shape = (block, quarter)
    source = lax.broadcasted_iota(jnp.int32, shape, 0) + pl.program_id(0) * block
    target = lax.broadcasted_iota(jnp.int32, shape, 1)
    apart = (target - source - shift_ref[0]) & (2 * quarter - 1)
    apart = jnp.where(apart >= quarter, apart - 2 * quarter, apart)
    near = jnp.where(apart > quarter // 2, quarter - apart, apart)
    near = jnp.where(apart < -(quarter // 2), -quarter - apart, near)
    u = near.astype(jnp.float32) * (math.pi / quarter)
    w = u * u
    poly = jnp.full(shape, 1.0 / 6227020800.0, jnp.float32)
    for c in (-1.0 / 39916800.0, 1.0 / 362880.0, -1.0 / 5040.0, 1.0 / 120.0, -1.0 / 6.0):
        poly = poly * w + c
    sine = u + u * (w * poly)
    zero = near == 0
    inverse = 0.25 / (quarter * jnp.where(zero, 1.0, sine))
    top_even = rows_ref[0:1, :] * cols_ref[:, 1:2] - rows_ref[1:2, :] * cols_ref[:, 0:1]
    top_half = rows_ref[2:3, :] * cols_ref[:, 3:4] - rows_ref[3:4, :] * cols_ref[:, 2:3]
    sign = jnp.where(apart == 0, 1.0, -1.0)
    m_even = jnp.where(zero, 0.25 * even / quarter, top_even * inverse)
    m_half = jnp.where(zero, sign * (0.25 * half / quarter), top_half * inverse)
    for value, high_ref, low_ref in ((m_even, eh_ref, el_ref), (m_half, hh_ref, hl_ref)):
        high = value.astype(jnp.bfloat16)
        high_ref[...] = high
        low_ref[...] = (value - high.astype(jnp.float32)).astype(jnp.bfloat16)


def filter_matrices(shift, tables, length):
    quarter = length // 4
    block = 128
    out = jax.ShapeDtypeStruct((quarter, quarter), jnp.bfloat16)
    return pl.pallas_call(
        lambda *refs: kernel_matrix_body(length, block, *refs),
        grid=(quarter // block,),
        out_shape=[out] * 4,
        in_specs=[
            pl.BlockSpec(memory_space=pltpu.SMEM),
            pl.BlockSpec((8, quarter), lambda i: (0, 0)),
            pl.BlockSpec((block, 4), lambda i: (i, 0)),
        ],
        out_specs=[pl.BlockSpec((block, quarter), lambda i: (i, 0))] * 4,
        compiler_params=pltpu.CompilerParams(vmem_limit_bytes=32 * MIB),
        cost_estimate=pl.CostEstimate(flops=60 * quarter * quarter, bytes_accessed=8 * quarter * quarter, transcendentals=0),
        name="filter_matrices",
    )(shift, tables, source_tables(length))


def split(value):
    high = value.astype(jnp.bfloat16)
    return high, (value - high.astype(jnp.float32)).astype(jnp.bfloat16)


def product(value, high_ref, low_ref):
    high, low = split(value)
    f32 = jnp.float32
    return (
        jnp.dot(high, low_ref[...], preferred_element_type=f32)
        + jnp.dot(low, high_ref[...], preferred_element_type=f32)
        + jnp.dot(high, high_ref[...], preferred_element_type=f32)
    )


def filter_body(x_ref, tab_ref, eh_ref, el_ref, hh_ref, hl_ref, out_ref):
    count = x_ref.shape[1]
    x0, x1, x2, x3 = [x_ref[i] for i in range(4)]
    cos_t, sin_t = 2.0 * tab_ref[4:5, :], 2.0 * tab_ref[5:6, :]
    cos_s, sin_s = tab_ref[6:7, :], tab_ref[7:8, :]
    even, odd = x0 + x2, x1 + x3
    re, im = x0 - x2, x3 - x1
    stacked = jnp.concatenate([even + odd, re * cos_s + im * sin_s, im * cos_s - re * sin_s], axis=0)
    turned = product(stacked, eh_ref, el_ref)
    z2 = product(even - odd, hh_ref, hl_ref)
    z0, ure, uim = turned[:count], turned[count : 2 * count], turned[2 * count :]
    zre = cos_t * ure - sin_t * uim
    zim = cos_t * uim + sin_t * ure
    plus, minus = z0 + z2, z0 - z2
    out_ref[0] = plus + zre
    out_ref[1] = minus - zim
    out_ref[2] = plus - zre
    out_ref[3] = minus + zim


def filtered(quarters, tables, matrices):
    _, count, quarter = quarters.shape
    block = next((b for b in (80, 64, 40, 32, 16, 8) if count % b == 0), count)
    whole = pl.BlockSpec((quarter, quarter), lambda i: (0, 0))
    part = pl.BlockSpec((4, block, quarter), lambda i: (0, i, 0))
    return pl.pallas_call(
        filter_body,
        grid=(count // block,),
        out_shape=jax.ShapeDtypeStruct(quarters.shape, jnp.float32),
        in_specs=[part, pl.BlockSpec((8, quarter), lambda i: (0, 0))] + [whole] * 4,
        out_specs=part,
        compiler_params=pltpu.CompilerParams(vmem_limit_bytes=48 * MIB),
        cost_estimate=pl.CostEstimate(
            flops=24 * count * quarter * quarter,
            bytes_accessed=32 * count * quarter + 8 * quarter * quarter,
            transcendentals=0,
        ),
        name="spectral_filter",
    )(quarters, tables, *matrices)


def to_quarters(pieces):
    sectors, count, sector = pieces.shape
    per = sectors // 4
    if per == 1:
        return pieces
    return pieces.reshape(4, per, count, sector).transpose(0, 2, 1, 3).reshape(4, count, per * sector)


def to_sectors(quarters, sectors):
    _, count, quarter = quarters.shape
    per = sectors // 4
    if per == 1:
        return quarters
    sector = quarter // per
    return quarters.reshape(4, count, per, sector).transpose(0, 2, 1, 3).reshape(sectors, count, sector)


def shifted(array, axis, dim, width):
    devices, length = (lax.axis_size(axis), array.shape[dim])
    up = [(i, (i + 1) % devices) for i in range(devices - 1)]
    down = [(j, i) for i, j in up]
    last = lax.slice_in_dim(array, length - width, length, axis=dim)
    leading = lax.slice_in_dim(array, 0, width, axis=dim)
    return lax.ppermute(last, axis, up), lax.ppermute(leading, axis, down)


def on_device(cycle, field, shift, owner):
    layers, variables, radial, sector = cycle.shape
    sectors = lax.axis_size("az")
    length = sectors * sector
    shift_value = shift[0]
    rows = layers * variables * radial
    piece = lax.all_to_all(cycle.reshape(sectors, rows // sectors, sector), "az", split_axis=0, concat_axis=0, tiled=True)
    tables = shift_tables(shift_value, length)
    matrices = filter_matrices(shift, tables, length)

    weights = jnp.array(LAYER_WEIGHTS, jnp.float32)
    cells = radial // KR
    grouped = cycle.reshape(layers, variables, cells, KR, sector)
    mean = jnp.sum(jnp.sum(grouped * weights[:, None, None, None, None], axis=0), axis=2) / KR
    around = lax.all_gather(mean.reshape(variables * cells, sector), "az", axis=0, tiled=False)
    ghost_all = to_sectors(filtered(to_quarters(around), tables, matrices), sectors)
    ghost = lax.dynamic_index_in_dim(ghost_all, lax.axis_index("az"), 0, keepdims=False)
    ghost = lax.all_gather(ghost.reshape(variables, cells, sector), "ax", axis=1, tiled=True)

    moved = to_sectors(filtered(to_quarters(piece), tables, matrices), sectors)
    shifted_cycle = lax.all_to_all(moved, "az", split_axis=0, concat_axis=0, tiled=True)
    shifted_cycle = shifted_cycle.reshape(layers, variables, radial, sector)

    mask = owner.astype(jnp.float32)[None, :, :, None]
    speeds = jnp.array(AXIAL_SPEEDS, jnp.float32)[:, None, None, None]
    at_inlet = lax.axis_index("ax") == 0

    def rates(state):
        inner, outer = shifted(state, "rad", 1, 1)
        under, over = shifted(state, "ax", 2, 1)
        lower = jnp.where(at_inlet, ghost[:, :, None], under)
        outward = jnp.concatenate([state[:, 1:], outer], axis=1)
        inward = jnp.concatenate([inner, state[:, :-1]], axis=1)
        above = jnp.concatenate([state[:, :, 1:], over], axis=2)
        below = jnp.concatenate([lower, state[:, :, :-1]], axis=2)
        return mask * (
            DIFFUSION * (outward + inward + above + below - 4.0 * state)
            - 0.5 * speeds * (above - below)
            - 0.5 * SWIRL_SPEED * (outward - inward)
        )

    first = rates(field)
    second = rates(field + 0.5 * first)
    third = rates(field + 0.5 * second)
    fourth = rates(field + third)
    field_next = field + (first + 2.0 * second + 2.0 * third + fourth) / 6.0
    return (field_next, shifted_cycle)


def solution(mesh):
    in_specs = (P(None, None, ("rad", "ax"), "az"), P(None, "rad", "ax", "az"), P(), P("rad", "ax"))
    out_specs = (P(None, "rad", "ax", "az"), P(None, None, ("rad", "ax"), "az"))
    return jax.shard_map(
        on_device, mesh=mesh, in_specs=in_specs, out_specs=out_specs, check_vma=False
    )
```

```python
import math

import jax
import jax.numpy as jnp
import numpy as np
from jax import lax
from jax.experimental import pallas as pl
from jax.experimental.pallas import tpu as pltpu
from jax.sharding import PartitionSpec as P

KR = 8


LAYER_WEIGHTS = (0.4, 0.3, 0.2, 0.1)
AXIAL_SPEEDS = (0.35, 0.2, 0.3, 0.25, 0.4)
DIFFUSION = 0.15
SWIRL_SPEED = 0.1
MIB = 1024 * 1024


def class_counts(length):
    top = (length - 1) // 3
    kept = np.arange(-top, top + 1)
    first = kept[kept % 4 == 1]
    assert length % 4 == 0 and (first - 1).sum() == 0
    even, odd, half = [int((kept % 4 == r).sum()) for r in (0, 1, 2)]
    assert even == odd
    return even, half


def shift_tables(shift_value, length):
    quarter = length // 4
    even, half = class_counts(length)
    target = jnp.arange(quarter, dtype=jnp.int32) - shift_value
    rows = []
    for count in (even, half):
        angle = jnp.remainder(count * target, 2 * quarter).astype(jnp.float32) * (math.pi / quarter)
        rows += [jnp.sin(angle), jnp.cos(angle)]
    angle = jnp.remainder(target, length).astype(jnp.float32) * (2.0 * math.pi / length)
    rows += [jnp.cos(angle), jnp.sin(angle)]
    source = np.arange(quarter) * (2.0 * np.pi / length)
    rows += [jnp.asarray(np.cos(source), jnp.float32), jnp.asarray(np.sin(source), jnp.float32)]
    return jnp.stack(rows)


def source_tables(length):
    quarter = length // 4
    source = np.arange(quarter)
    cols = []
    for count in class_counts(length):
        angle = (count * source % (2 * quarter)) * (np.pi / quarter)
        cols += [np.sin(angle), np.cos(angle)]
    return jnp.asarray(np.stack(cols, axis=1), jnp.float32)


def kernel_matrix_body(length, block, shift_ref, rows_ref, cols_ref, eh_ref, el_ref, hh_ref, hl_ref):
    quarter = length // 4
    even, half = class_counts(length)
    shape = (block, quarter)
    source = lax.broadcasted_iota(jnp.int32, shape, 0) + pl.program_id(0) * block
    target = lax.broadcasted_iota(jnp.int32, shape, 1)
    apart = (target - source - shift_ref[0]) & (2 * quarter - 1)
    apart = jnp.where(apart >= quarter, apart - 2 * quarter, apart)
    near = jnp.where(apart > quarter // 2, quarter - apart, apart)
    near = jnp.where(apart < -(quarter // 2), -quarter - apart, near)
    u = near.astype(jnp.float32) * (math.pi / quarter)
    w = u * u
    poly = jnp.full(shape, 1.0 / 6227020800.0, jnp.float32)
    for c in (-1.0 / 39916800.0, 1.0 / 362880.0, -1.0 / 5040.0, 1.0 / 120.0, -1.0 / 6.0):
        poly = poly * w + c
    sine = u + u * (w * poly)
    zero = near == 0
    inverse = 0.25 / (quarter * jnp.where(zero, 1.0, sine))
    top_even = rows_ref[0:1, :] * cols_ref[:, 1:2] - rows_ref[1:2, :] * cols_ref[:, 0:1]
    top_half = rows_ref[2:3, :] * cols_ref[:, 3:4] - rows_ref[3:4, :] * cols_ref[:, 2:3]
    sign = jnp.where(apart == 0, 1.0, -1.0)
    m_even = jnp.where(zero, 0.25 * even / quarter, top_even * inverse)
    m_half = jnp.where(zero, sign * (0.25 * half / quarter), top_half * inverse)
    for value, high_ref, low_ref in ((m_even, eh_ref, el_ref), (m_half, hh_ref, hl_ref)):
        high = value.astype(jnp.bfloat16)
        high_ref[...] = high
        low_ref[...] = (value - high.astype(jnp.float32)).astype(jnp.bfloat16)


def filter_matrices(shift, tables, length):
    quarter = length // 4
    block = 128
    out = jax.ShapeDtypeStruct((quarter, quarter), jnp.bfloat16)
    return pl.pallas_call(
        lambda *refs: kernel_matrix_body(length, block, *refs),
        grid=(quarter // block,),
        out_shape=[out] * 4,
        in_specs=[
            pl.BlockSpec(memory_space=pltpu.SMEM),
            pl.BlockSpec((8, quarter), lambda i: (0, 0)),
            pl.BlockSpec((block, 4), lambda i: (i, 0)),
        ],
        out_specs=[pl.BlockSpec((block, quarter), lambda i: (i, 0))] * 4,
        compiler_params=pltpu.CompilerParams(vmem_limit_bytes=32 * MIB),
        cost_estimate=pl.CostEstimate(flops=60 * quarter * quarter, bytes_accessed=8 * quarter * quarter, transcendentals=0),
        name="filter_matrices",
    )(shift, tables, source_tables(length))


def split(value):
    high = value.astype(jnp.bfloat16)
    return high, (value - high.astype(jnp.float32)).astype(jnp.bfloat16)


def product(value, high_ref, low_ref):
    high, low = split(value)
    f32 = jnp.float32
    return (
        jnp.dot(high, low_ref[...], preferred_element_type=f32)
        + jnp.dot(low, high_ref[...], preferred_element_type=f32)
        + jnp.dot(high, high_ref[...], preferred_element_type=f32)
    )


def filter_body(x_ref, tab_ref, eh_ref, el_ref, hh_ref, hl_ref, out_ref):
    count = x_ref.shape[1]
    x0, x1, x2, x3 = [x_ref[i] for i in range(4)]
    cos_t, sin_t = 2.0 * tab_ref[4:5, :], 2.0 * tab_ref[5:6, :]
    cos_s, sin_s = tab_ref[6:7, :], tab_ref[7:8, :]
    even, odd = x0 + x2, x1 + x3
    re, im = x0 - x2, x3 - x1
    stacked = jnp.concatenate([even + odd, re * cos_s + im * sin_s, im * cos_s - re * sin_s], axis=0)
    turned = product(stacked, eh_ref, el_ref)
    z2 = product(even - odd, hh_ref, hl_ref)
    z0, ure, uim = turned[:count], turned[count : 2 * count], turned[2 * count :]
    zre = cos_t * ure - sin_t * uim
    zim = cos_t * uim + sin_t * ure
    plus, minus = z0 + z2, z0 - z2
    out_ref[0] = plus + zre
    out_ref[1] = minus - zim
    out_ref[2] = plus - zre
    out_ref[3] = minus + zim


def filtered(quarters, tables, matrices):
    _, count, quarter = quarters.shape
    block = next((b for b in (80, 64, 40, 32, 16, 8) if count % b == 0), count)
    whole = pl.BlockSpec((quarter, quarter), lambda i: (0, 0))
    part = pl.BlockSpec((4, block, quarter), lambda i: (0, i, 0))
    return pl.pallas_call(
        filter_body,
        grid=(count // block,),
        out_shape=jax.ShapeDtypeStruct(quarters.shape, jnp.float32),
        in_specs=[part, pl.BlockSpec((8, quarter), lambda i: (0, 0))] + [whole] * 4,
        out_specs=part,
        compiler_params=pltpu.CompilerParams(vmem_limit_bytes=48 * MIB),
        cost_estimate=pl.CostEstimate(
            flops=24 * count * quarter * quarter,
            bytes_accessed=32 * count * quarter + 8 * quarter * quarter,
            transcendentals=0,
        ),
        name="spectral_filter",
    )(quarters, tables, *matrices)


def to_quarters(pieces):
    sectors, count, sector = pieces.shape
    per = sectors // 4
    if per == 1:
        return pieces
    return pieces.reshape(4, per, count, sector).transpose(0, 2, 1, 3).reshape(4, count, per * sector)


def to_sectors(quarters, sectors):
    _, count, quarter = quarters.shape
    per = sectors // 4
    if per == 1:
        return quarters
    sector = quarter // per
    return quarters.reshape(4, count, per, sector).transpose(0, 2, 1, 3).reshape(sectors, count, sector)


def shifted(array, axis, dim, width):
    devices, length = (lax.axis_size(axis), array.shape[dim])
    up = [(i, (i + 1) % devices) for i in range(devices - 1)]
    down = [(j, i) for i, j in up]
    last = lax.slice_in_dim(array, length - width, length, axis=dim)
    leading = lax.slice_in_dim(array, 0, width, axis=dim)
    return lax.ppermute(last, axis, up), lax.ppermute(leading, axis, down)


def on_device(cycle, field, shift, owner):
    layers, variables, radial, sector = cycle.shape
    sectors = lax.axis_size("az")
    length = sectors * sector
    shift_value = shift[0]
    tables = shift_tables(shift_value, length)
    matrices = filter_matrices(shift, tables, length)

    def across(part):
        return lax.all_to_all(part, "az", split_axis=0, concat_axis=0, tiled=True)

    def passed(pieces):
        return to_sectors(filtered(to_quarters(pieces), tables, matrices), sectors)

    lead = cycle[:1].reshape(sectors, -1, sector)
    rest = cycle[1:].reshape(sectors, -1, sector)
    lead = across(lead)

    weights = jnp.array(LAYER_WEIGHTS, jnp.float32)
    cells = radial // KR
    grouped = cycle.reshape(layers, variables, cells, KR, sector)
    mean = jnp.sum(jnp.sum(grouped * weights[:, None, None, None, None], axis=0), axis=2) / KR
    around = lax.all_gather(mean.reshape(variables * cells, sector), "az", axis=0, tiled=False)
    lead, around, rest = lax.optimization_barrier((lead, around, rest))
    rest = across(rest)

    ghost = lax.dynamic_index_in_dim(passed(around), lax.axis_index("az"), 0, keepdims=False)
    ghost = lax.all_gather(ghost.reshape(variables, cells, sector), "ax", axis=1, tiled=True)

    lead, rest = lax.optimization_barrier((passed(lead), rest))
    lead = across(lead).reshape(1, variables, radial, sector)
    rest = across(passed(rest)).reshape(layers - 1, variables, radial, sector)
    shifted_cycle = jnp.concatenate([lead, rest], axis=0)

    mask = owner.astype(jnp.float32)[None, :, :, None]
    speeds = jnp.array(AXIAL_SPEEDS, jnp.float32)[:, None, None, None]
    at_inlet = lax.axis_index("ax") == 0

    def rates(state):
        inner, outer = shifted(state, "rad", 1, 1)
        under, over = shifted(state, "ax", 2, 1)
        lower = jnp.where(at_inlet, ghost[:, :, None], under)
        outward = jnp.concatenate([state[:, 1:], outer], axis=1)
        inward = jnp.concatenate([inner, state[:, :-1]], axis=1)
        above = jnp.concatenate([state[:, :, 1:], over], axis=2)
        below = jnp.concatenate([lower, state[:, :, :-1]], axis=2)
        return mask * (
            DIFFUSION * (outward + inward + above + below - 4.0 * state)
            - 0.5 * speeds * (above - below)
            - 0.5 * SWIRL_SPEED * (outward - inward)
        )

    first = rates(field)
    second = rates(field + 0.5 * first)
    third = rates(field + 0.5 * second)
    fourth = rates(field + third)
    field_next = field + (first + 2.0 * second + 2.0 * third + fourth) / 6.0
    return (field_next, shifted_cycle)


def solution(mesh):
    in_specs = (P(None, None, ("rad", "ax"), "az"), P(None, "rad", "ax", "az"), P(), P("rad", "ax"))
    out_specs = (P(None, "rad", "ax", "az"), P(None, None, ("rad", "ax"), "az"))
    return jax.shard_map(
        on_device, mesh=mesh, in_specs=in_specs, out_specs=out_specs, check_vma=False
    )
```

```python
import math

import jax
import jax.numpy as jnp
import numpy as np
from jax import lax
from jax.experimental import pallas as pl
from jax.experimental.pallas import tpu as pltpu
from jax.sharding import PartitionSpec as P

KR = 8


LAYER_WEIGHTS = (0.4, 0.3, 0.2, 0.1)
AXIAL_SPEEDS = (0.35, 0.2, 0.3, 0.25, 0.4)
DIFFUSION = 0.15
SWIRL_SPEED = 0.1
MIB = 1024 * 1024


def class_counts(length):
    top = (length - 1) // 3
    kept = np.arange(-top, top + 1)
    first = kept[kept % 4 == 1]
    assert length % 4 == 0 and (first - 1).sum() == 0
    even, odd, half = [int((kept % 4 == r).sum()) for r in (0, 1, 2)]
    assert even == odd
    return even, half


def shift_tables(shift_value, length):
    quarter = length // 4
    even, half = class_counts(length)
    target = jnp.arange(quarter, dtype=jnp.int32) - shift_value
    rows = []
    for count in (even, half):
        angle = jnp.remainder(count * target, 2 * quarter).astype(jnp.float32) * (math.pi / quarter)
        rows += [jnp.sin(angle), jnp.cos(angle)]
    angle = jnp.remainder(target, length).astype(jnp.float32) * (2.0 * math.pi / length)
    rows += [jnp.cos(angle), jnp.sin(angle)]
    source = np.arange(quarter) * (2.0 * np.pi / length)
    rows += [jnp.asarray(np.cos(source), jnp.float32), jnp.asarray(np.sin(source), jnp.float32)]
    return jnp.stack(rows)


def source_tables(length):
    quarter = length // 4
    source = np.arange(quarter)
    cols = []
    for count in class_counts(length):
        angle = (count * source % (2 * quarter)) * (np.pi / quarter)
        cols += [np.sin(angle), np.cos(angle)]
    return jnp.asarray(np.stack(cols, axis=1), jnp.float32)


def matrix_values(length, first, block, shift_value, rows, cols):
    quarter = length // 4
    even, half = class_counts(length)
    shape = (block, quarter)
    source = lax.broadcasted_iota(jnp.int32, shape, 0) + first
    target = lax.broadcasted_iota(jnp.int32, shape, 1)
    apart = (target - source - shift_value) & (2 * quarter - 1)
    apart = jnp.where(apart >= quarter, apart - 2 * quarter, apart)
    near = jnp.where(apart > quarter // 2, quarter - apart, apart)
    near = jnp.where(apart < -(quarter // 2), -quarter - apart, near)
    u = near.astype(jnp.float32) * (math.pi / quarter)
    w = u * u
    poly = jnp.full(shape, 1.0 / 6227020800.0, jnp.float32)
    for c in (-1.0 / 39916800.0, 1.0 / 362880.0, -1.0 / 5040.0, 1.0 / 120.0, -1.0 / 6.0):
        poly = poly * w + c
    sine = u + u * (w * poly)
    zero = near == 0
    inverse = 0.25 / (quarter * jnp.where(zero, 1.0, sine))
    top_even = rows[0:1, :] * cols[:, 1:2] - rows[1:2, :] * cols[:, 0:1]
    top_half = rows[2:3, :] * cols[:, 3:4] - rows[3:4, :] * cols[:, 2:3]
    sign = jnp.where(apart == 0, 1.0, -1.0)
    m_even = jnp.where(zero, 0.25 * even / quarter, top_even * inverse)
    m_half = jnp.where(zero, sign * (0.25 * half / quarter), top_half * inverse)
    return split(m_even) + split(m_half)


def kernel_matrix_body(length, block, shift_ref, rows_ref, cols_ref, *out_refs):
    first = pl.program_id(0) * block
    values = matrix_values(length, first, block, shift_ref[0], rows_ref[...], cols_ref[...])
    for ref, value in zip(out_refs, values):
        ref[...] = value


def filter_matrices(shift, tables, length):
    quarter = length // 4
    block = 128
    out = jax.ShapeDtypeStruct((quarter, quarter), jnp.bfloat16)
    return pl.pallas_call(
        lambda *refs: kernel_matrix_body(length, block, *refs),
        grid=(quarter // block,),
        out_shape=[out] * 4,
        in_specs=[
            pl.BlockSpec(memory_space=pltpu.SMEM),
            pl.BlockSpec((8, quarter), lambda i: (0, 0)),
            pl.BlockSpec((block, 4), lambda i: (i, 0)),
        ],
        out_specs=[pl.BlockSpec((block, quarter), lambda i: (i, 0))] * 4,
        compiler_params=pltpu.CompilerParams(vmem_limit_bytes=32 * MIB),
        cost_estimate=pl.CostEstimate(flops=60 * quarter * quarter, bytes_accessed=8 * quarter * quarter, transcendentals=0),
        name="filter_matrices",
    )(shift, tables, source_tables(length))


def split(value):
    high = value.astype(jnp.bfloat16)
    return high, (value - high.astype(jnp.float32)).astype(jnp.bfloat16)


def product(value, high_ref, low_ref):
    high, low = split(value)
    f32 = jnp.float32
    return (
        jnp.dot(high, low_ref[...], preferred_element_type=f32)
        + jnp.dot(low, high_ref[...], preferred_element_type=f32)
        + jnp.dot(high, high_ref[...], preferred_element_type=f32)
    )


def filter_quarters(parts, tab_ref, matrix_refs):
    x0, x1, x2, x3 = parts
    count = x0.shape[0]
    eh_ref, el_ref, hh_ref, hl_ref = matrix_refs
    cos_t, sin_t = 2.0 * tab_ref[4:5, :], 2.0 * tab_ref[5:6, :]
    cos_s, sin_s = tab_ref[6:7, :], tab_ref[7:8, :]
    even, odd = x0 + x2, x1 + x3
    re, im = x0 - x2, x3 - x1
    stacked = jnp.concatenate([even + odd, re * cos_s + im * sin_s, im * cos_s - re * sin_s], axis=0)
    turned = product(stacked, eh_ref, el_ref)
    z2 = product(even - odd, hh_ref, hl_ref)
    z0, ure, uim = turned[:count], turned[count : 2 * count], turned[2 * count :]
    zre = cos_t * ure - sin_t * uim
    zim = cos_t * uim + sin_t * ure
    plus, minus = z0 + z2, z0 - z2
    return plus + zre, minus - zim, plus - zre, minus + zim


def filter_body(x_ref, tab_ref, eh_ref, el_ref, hh_ref, hl_ref, out_ref):
    values = filter_quarters([x_ref[i] for i in range(4)], tab_ref, (eh_ref, el_ref, hh_ref, hl_ref))
    for i, value in enumerate(values):
        out_ref[i] = value


def filtered(quarters, tables, matrices):
    _, count, quarter = quarters.shape
    block = next((b for b in (80, 64, 40, 32, 16, 8) if count % b == 0), count)
    whole = pl.BlockSpec((quarter, quarter), lambda i: (0, 0))
    part = pl.BlockSpec((4, block, quarter), lambda i: (0, i, 0))
    return pl.pallas_call(
        filter_body,
        grid=(count // block,),
        out_shape=jax.ShapeDtypeStruct(quarters.shape, jnp.float32),
        in_specs=[part, pl.BlockSpec((8, quarter), lambda i: (0, 0))] + [whole] * 4,
        out_specs=part,
        compiler_params=pltpu.CompilerParams(vmem_limit_bytes=48 * MIB),
        cost_estimate=pl.CostEstimate(
            flops=24 * count * quarter * quarter,
            bytes_accessed=32 * count * quarter + 8 * quarter * quarter,
            transcendentals=0,
        ),
        name="spectral_filter",
    )(quarters, tables, *matrices)


def to_quarters(pieces):
    sectors, count, sector = pieces.shape
    per = sectors // 4
    if per == 1:
        return pieces
    return pieces.reshape(4, per, count, sector).transpose(0, 2, 1, 3).reshape(4, count, per * sector)


def to_sectors(quarters, sectors):
    _, count, quarter = quarters.shape
    per = sectors // 4
    if per == 1:
        return quarters
    sector = quarter // per
    return quarters.reshape(4, count, per, sector).transpose(0, 2, 1, 3).reshape(sectors, count, sector)


def still_tables(length):
    quarter = length // 4
    target = np.arange(quarter)
    rows = []
    for count in class_counts(length):
        angle = (count * target % (2 * quarter)) * (np.pi / quarter)
        rows += [np.sin(angle), np.cos(angle)]
    angle = target * (2.0 * np.pi / length)
    rows += [np.cos(angle), np.sin(angle)] * 2
    return jnp.asarray(np.stack(rows), jnp.float32)


def turn_values(shift_value, length):
    quarter = length // 4
    even, half = class_counts(length)
    steps = jnp.array([2 * even, 2 * half, 1], jnp.int32) * shift_value
    angle = jnp.remainder(steps, length).astype(jnp.float32) * (2.0 * math.pi / length)
    return jnp.concatenate([jnp.sin(angle), jnp.cos(angle)])


def forward_body(length, block, cells, turn_ref, shift_ref, rows_ref, cols_ref, cycle_ref, out_ref, ghost_ref,
                 land, done, local, mean, ghosts, eh, el, hh, hl, tab, send_sem, recv_sem, mean_send, mean_recv, local_sem, store_sem):
    count = land.shape[1]
    chunks = count // block
    quarter = length // 4
    me = lax.axis_index("az")
    matrices = (eh, el, hh, hl)

    barrier = pltpu.get_barrier_semaphore()
    for k in (1, 2, 3):
        pl.semaphore_signal(barrier, inc=1, device_id={"az": lax.rem(me + k, 4)}, device_id_type=pl.DeviceIdType.MESH)
    pl.semaphore_wait(barrier, 3)

    def part(c):
        return pl.ds(pl.multiple_of(c * block, block), block)

    def send(c, k):
        peer = lax.rem(me + k, 4)
        return pltpu.make_async_remote_copy(
            src_ref=cycle_ref.at[peer, part(c)],
            dst_ref=land.at[me, part(c)],
            send_sem=send_sem.at[c, k - 1],
            recv_sem=recv_sem.at[c, k - 1],
            device_id={"az": peer},
            device_id_type=pl.DeviceIdType.MESH,
        )

    def send_mean(k):
        return pltpu.make_async_remote_copy(
            src_ref=mean.at[me],
            dst_ref=mean.at[me],
            send_sem=mean_send.at[k - 1],
            recv_sem=mean_recv.at[k - 1],
            device_id={"az": lax.rem(me + k, 4)},
            device_id_type=pl.DeviceIdType.MESH,
        )

    def store(c):
        return pltpu.make_async_copy(done.at[:, part(c)], out_ref.at[:, part(c)], store_sem.at[c])

    whole = pltpu.make_async_copy(cycle_ref, local, local_sem.at[0])
    own = pltpu.make_async_copy(cycle_ref.at[me], land.at[me], local_sem.at[1])
    for c in (0, 1):
        for k in (2, 1, 3):
            send(c, k).start()
    whole.start()
    own.start()

    whole.wait()

    def average(c, carry):
        rows = pl.ds(pl.multiple_of(c * 8 * KR, 8 * KR), 8 * KR)
        total = LAYER_WEIGHTS[0] * local[0, rows]
        for layer in (1, 2, 3):
            total = total + LAYER_WEIGHTS[layer] * local[layer, rows]
        mean[me, pl.ds(pl.multiple_of(c * 8, 8), 8)] = jnp.sum(total.reshape(8, KR, quarter), axis=1) / KR
        return carry

    lax.fori_loop(0, cells // 8, average, 0)
    for k in (2, 1, 3):
        send_mean(k).start()

    tab[...] = rows_ref[...]
    for at, turn in ((0, 0), (2, 1)):
        sine, cosine = rows_ref[at : at + 1, :], rows_ref[at + 1 : at + 2, :]
        tab[at : at + 1, :] = sine * turn_ref[3 + turn] - cosine * turn_ref[turn]
        tab[at + 1 : at + 2, :] = cosine * turn_ref[3 + turn] + sine * turn_ref[turn]
    cosine, sine = rows_ref[4:5, :], rows_ref[5:6, :]
    tab[4:5, :] = cosine * turn_ref[5] + sine * turn_ref[2]
    tab[5:6, :] = sine * turn_ref[5] - cosine * turn_ref[2]

    def build(i, carry):
        first = pl.multiple_of(i * 128, 128)
        rows = pl.ds(first, 128)
        values = matrix_values(length, first, 128, shift_ref[0], tab[...], cols_ref[rows, :])
        for ref, value in zip(matrices, values):
            ref[rows, :] = value
        return carry

    lax.fori_loop(0, quarter // 128, build, 0)
    own.wait()

    def step(c, carry):
        for k in (2, 1, 3):
            send(c, k).wait_recv()

        @pl.when(c + 2 < chunks)
        def _():
            for k in (2, 1, 3):
                send(c + 2, k).start()

        values = filter_quarters([land[i, part(c)] for i in range(4)], tab, matrices)
        for i, value in enumerate(values):
            done[i, part(c)] = value
        store(c).start()
        return carry

    lax.fori_loop(0, chunks, step, 0)

    for k in (1, 2, 3):
        send_mean(k).wait_recv()
    for i, value in enumerate(filter_quarters([mean[i] for i in range(4)], tab, matrices)):
        ghosts[i] = value
    ghost_ref[...] = ghosts[me]

    def finish(c, carry):
        for k in (1, 2, 3):
            send(c, k).wait_send()
        store(c).wait()
        return carry

    lax.fori_loop(0, chunks, finish, 0)
    for k in (1, 2, 3):
        send_mean(k).wait_send()


def forward(rows, shift, cells):
    sectors, count, sector = rows.shape
    length = sectors * sector
    block = 80
    chunks = count // block
    f32, bf16 = jnp.float32, jnp.bfloat16
    smem = pl.BlockSpec(memory_space=pltpu.SMEM)
    vmem = pl.BlockSpec(memory_space=pltpu.VMEM)
    hbm = pl.BlockSpec(memory_space=pl.ANY)
    dma = pltpu.SemaphoreType.DMA
    return pl.pallas_call(
        lambda *refs: forward_body(length, block, cells, *refs),
        out_shape=[jax.ShapeDtypeStruct(rows.shape, f32), jax.ShapeDtypeStruct((cells, sector), f32)],
        in_specs=[smem, smem, vmem, vmem, hbm],
        out_specs=[hbm, vmem],
        scratch_shapes=[pltpu.VMEM(rows.shape, f32)] * 3
        + [pltpu.VMEM((4, cells, sector), f32)] * 2
        + [pltpu.VMEM((sector, sector), bf16)] * 4
        + [pltpu.VMEM((8, sector), f32), dma((chunks, 3)), dma((chunks, 3)), dma((3,)), dma((3,)), dma((2,)), dma((chunks,))],
        compiler_params=pltpu.CompilerParams(vmem_limit_bytes=52 * MIB, collective_id=0, has_side_effects=True),
        cost_estimate=pl.CostEstimate(flops=24 * count * sector * sector, bytes_accessed=12 * count * length, transcendentals=0),
        name="forward_filter",
    )(turn_values(shift[0], length), shift, still_tables(length), source_tables(length), rows)


def shifted(array, axis, dim, width):
    devices, length = (lax.axis_size(axis), array.shape[dim])
    up = [(i, (i + 1) % devices) for i in range(devices - 1)]
    down = [(j, i) for i, j in up]
    last = lax.slice_in_dim(array, length - width, length, axis=dim)
    leading = lax.slice_in_dim(array, 0, width, axis=dim)
    return lax.ppermute(last, axis, up), lax.ppermute(leading, axis, down)


def chunked(cycle, shift):
    layers, variables, radial, sector = cycle.shape
    sectors = lax.axis_size("az")
    length = sectors * sector
    shift_value = shift[0]
    tables = shift_tables(shift_value, length)
    matrices = filter_matrices(shift, tables, length)

    def across(part):
        return lax.all_to_all(part, "az", split_axis=0, concat_axis=0, tiled=True)

    def passed(pieces):
        return to_sectors(filtered(to_quarters(pieces), tables, matrices), sectors)

    lead = cycle[:1].reshape(sectors, -1, sector)
    rest = cycle[1:].reshape(sectors, -1, sector)
    lead = across(lead)

    weights = jnp.array(LAYER_WEIGHTS, jnp.float32)
    cells = radial // KR
    grouped = cycle.reshape(layers, variables, cells, KR, sector)
    mean = jnp.sum(jnp.sum(grouped * weights[:, None, None, None, None], axis=0), axis=2) / KR
    around = lax.all_gather(mean.reshape(variables * cells, sector), "az", axis=0, tiled=False)
    lead, around, rest = lax.optimization_barrier((lead, around, rest))
    rest = across(rest)

    ghost = lax.dynamic_index_in_dim(passed(around), lax.axis_index("az"), 0, keepdims=False)

    lead, rest = lax.optimization_barrier((passed(lead), rest))
    lead = across(lead).reshape(1, variables, radial, sector)
    rest = across(passed(rest)).reshape(layers - 1, variables, radial, sector)
    shifted_cycle = jnp.concatenate([lead, rest], axis=0)
    return ghost, shifted_cycle


def on_device(cycle, field, shift, owner):
    layers, variables, radial, sector = cycle.shape
    sectors = lax.axis_size("az")
    cells = variables * (radial // KR)
    if sectors == layers == 4 and (variables * radial) % 160 == 0 and cells % 8 == 0:
        moved, ghost = forward(cycle.reshape(layers, variables * radial, sector), shift, cells)
        shifted_cycle = lax.all_to_all(moved, "az", split_axis=0, concat_axis=0, tiled=True).reshape(cycle.shape)
    else:
        ghost, shifted_cycle = chunked(cycle, shift)
    ghost = lax.all_gather(ghost.reshape(variables, radial // KR, sector), "ax", axis=1, tiled=True)

    mask = owner.astype(jnp.float32)[None, :, :, None]
    speeds = jnp.array(AXIAL_SPEEDS, jnp.float32)[:, None, None, None]
    at_inlet = lax.axis_index("ax") == 0

    def rates(state):
        inner, outer = shifted(state, "rad", 1, 1)
        under, over = shifted(state, "ax", 2, 1)
        lower = jnp.where(at_inlet, ghost[:, :, None], under)
        outward = jnp.concatenate([state[:, 1:], outer], axis=1)
        inward = jnp.concatenate([inner, state[:, :-1]], axis=1)
        above = jnp.concatenate([state[:, :, 1:], over], axis=2)
        below = jnp.concatenate([lower, state[:, :, :-1]], axis=2)
        return mask * (
            DIFFUSION * (outward + inward + above + below - 4.0 * state)
            - 0.5 * speeds * (above - below)
            - 0.5 * SWIRL_SPEED * (outward - inward)
        )

    first = rates(field)
    second = rates(field + 0.5 * first)
    third = rates(field + 0.5 * second)
    fourth = rates(field + third)
    field_next = field + (first + 2.0 * second + 2.0 * third + fourth) / 6.0
    return (field_next, shifted_cycle)


def solution(mesh):
    in_specs = (P(None, None, ("rad", "ax"), "az"), P(None, "rad", "ax", "az"), P(), P("rad", "ax"))
    out_specs = (P(None, "rad", "ax", "az"), P(None, None, ("rad", "ax"), "az"))
    return jax.shard_map(
        on_device, mesh=mesh, in_specs=in_specs, out_specs=out_specs, check_vma=False
    )
```

```python
import math

import jax
import jax.numpy as jnp
import numpy as np
from jax import lax
from jax.experimental import pallas as pl
from jax.experimental.pallas import tpu as pltpu
from jax.sharding import PartitionSpec as P

KR = 8


LAYER_WEIGHTS = (0.4, 0.3, 0.2, 0.1)
AXIAL_SPEEDS = (0.35, 0.2, 0.3, 0.25, 0.4)
DIFFUSION = 0.15
SWIRL_SPEED = 0.1
MIB = 1024 * 1024


def class_counts(length):
    top = (length - 1) // 3
    kept = np.arange(-top, top + 1)
    first = kept[kept % 4 == 1]
    assert length % 4 == 0 and (first - 1).sum() == 0
    even, odd, half = [int((kept % 4 == r).sum()) for r in (0, 1, 2)]
    assert even == odd
    return even, half


def shift_tables(shift_value, length):
    quarter = length // 4
    even, half = class_counts(length)
    target = jnp.arange(quarter, dtype=jnp.int32) - shift_value
    rows = []
    for count in (even, half):
        angle = jnp.remainder(count * target, 2 * quarter).astype(jnp.float32) * (math.pi / quarter)
        rows += [jnp.sin(angle), jnp.cos(angle)]
    angle = jnp.remainder(target, length).astype(jnp.float32) * (2.0 * math.pi / length)
    rows += [jnp.cos(angle), jnp.sin(angle)]
    source = np.arange(quarter) * (2.0 * np.pi / length)
    rows += [jnp.asarray(np.cos(source), jnp.float32), jnp.asarray(np.sin(source), jnp.float32)]
    return jnp.stack(rows)


def source_tables(length):
    quarter = length // 4
    source = np.arange(quarter)
    cols = []
    for count in class_counts(length):
        angle = (count * source % (2 * quarter)) * (np.pi / quarter)
        cols += [np.sin(angle), np.cos(angle)]
    return jnp.asarray(np.stack(cols, axis=1), jnp.float32)


def matrix_values(length, first, block, shift_value, rows, cols):
    quarter = length // 4
    even, half = class_counts(length)
    shape = (block, quarter)
    source = lax.broadcasted_iota(jnp.int32, shape, 0) + first
    target = lax.broadcasted_iota(jnp.int32, shape, 1)
    apart = (target - source - shift_value) & (2 * quarter - 1)
    apart = jnp.where(apart >= quarter, apart - 2 * quarter, apart)
    near = jnp.where(apart > quarter // 2, quarter - apart, apart)
    near = jnp.where(apart < -(quarter // 2), -quarter - apart, near)
    u = near.astype(jnp.float32) * (math.pi / quarter)
    w = u * u
    poly = jnp.full(shape, 1.0 / 6227020800.0, jnp.float32)
    for c in (-1.0 / 39916800.0, 1.0 / 362880.0, -1.0 / 5040.0, 1.0 / 120.0, -1.0 / 6.0):
        poly = poly * w + c
    sine = u + u * (w * poly)
    zero = near == 0
    inverse = 0.25 / (quarter * jnp.where(zero, 1.0, sine))
    top_even = rows[0:1, :] * cols[:, 1:2] - rows[1:2, :] * cols[:, 0:1]
    top_half = rows[2:3, :] * cols[:, 3:4] - rows[3:4, :] * cols[:, 2:3]
    sign = jnp.where(apart == 0, 1.0, -1.0)
    m_even = jnp.where(zero, 0.25 * even / quarter, top_even * inverse)
    m_half = jnp.where(zero, sign * (0.25 * half / quarter), top_half * inverse)
    return split(m_even) + split(m_half)


def kernel_matrix_body(length, block, shift_ref, rows_ref, cols_ref, *out_refs):
    first = pl.program_id(0) * block
    values = matrix_values(length, first, block, shift_ref[0], rows_ref[...], cols_ref[...])
    for ref, value in zip(out_refs, values):
        ref[...] = value


def filter_matrices(shift, tables, length):
    quarter = length // 4
    block = 128
    out = jax.ShapeDtypeStruct((quarter, quarter), jnp.bfloat16)
    return pl.pallas_call(
        lambda *refs: kernel_matrix_body(length, block, *refs),
        grid=(quarter // block,),
        out_shape=[out] * 4,
        in_specs=[
            pl.BlockSpec(memory_space=pltpu.SMEM),
            pl.BlockSpec((8, quarter), lambda i: (0, 0)),
            pl.BlockSpec((block, 4), lambda i: (i, 0)),
        ],
        out_specs=[pl.BlockSpec((block, quarter), lambda i: (i, 0))] * 4,
        compiler_params=pltpu.CompilerParams(vmem_limit_bytes=32 * MIB),
        cost_estimate=pl.CostEstimate(flops=60 * quarter * quarter, bytes_accessed=8 * quarter * quarter, transcendentals=0),
        name="filter_matrices",
    )(shift, tables, source_tables(length))


def split(value):
    high = value.astype(jnp.bfloat16)
    return high, (value - high.astype(jnp.float32)).astype(jnp.bfloat16)


def product(value, high_ref, low_ref):
    high, low = split(value)
    f32 = jnp.float32
    return (
        jnp.dot(high, low_ref[...], preferred_element_type=f32)
        + jnp.dot(low, high_ref[...], preferred_element_type=f32)
        + jnp.dot(high, high_ref[...], preferred_element_type=f32)
    )


def filter_quarters(parts, tab_ref, matrix_refs):
    x0, x1, x2, x3 = parts
    count = x0.shape[0]
    eh_ref, el_ref, hh_ref, hl_ref = matrix_refs
    cos_t, sin_t = 2.0 * tab_ref[4:5, :], 2.0 * tab_ref[5:6, :]
    cos_s, sin_s = tab_ref[6:7, :], tab_ref[7:8, :]
    even, odd = x0 + x2, x1 + x3
    re, im = x0 - x2, x3 - x1
    stacked = jnp.concatenate([even + odd, re * cos_s + im * sin_s, im * cos_s - re * sin_s], axis=0)
    turned = product(stacked, eh_ref, el_ref)
    z2 = product(even - odd, hh_ref, hl_ref)
    z0, ure, uim = turned[:count], turned[count : 2 * count], turned[2 * count :]
    zre = cos_t * ure - sin_t * uim
    zim = cos_t * uim + sin_t * ure
    plus, minus = z0 + z2, z0 - z2
    return plus + zre, minus - zim, plus - zre, minus + zim


def filter_body(x_ref, tab_ref, eh_ref, el_ref, hh_ref, hl_ref, out_ref):
    values = filter_quarters([x_ref[i] for i in range(4)], tab_ref, (eh_ref, el_ref, hh_ref, hl_ref))
    for i, value in enumerate(values):
        out_ref[i] = value


def filtered(quarters, tables, matrices):
    _, count, quarter = quarters.shape
    block = next((b for b in (80, 64, 40, 32, 16, 8) if count % b == 0), count)
    whole = pl.BlockSpec((quarter, quarter), lambda i: (0, 0))
    part = pl.BlockSpec((4, block, quarter), lambda i: (0, i, 0))
    return pl.pallas_call(
        filter_body,
        grid=(count // block,),
        out_shape=jax.ShapeDtypeStruct(quarters.shape, jnp.float32),
        in_specs=[part, pl.BlockSpec((8, quarter), lambda i: (0, 0))] + [whole] * 4,
        out_specs=part,
        compiler_params=pltpu.CompilerParams(vmem_limit_bytes=48 * MIB),
        cost_estimate=pl.CostEstimate(
            flops=24 * count * quarter * quarter,
            bytes_accessed=32 * count * quarter + 8 * quarter * quarter,
            transcendentals=0,
        ),
        name="spectral_filter",
    )(quarters, tables, *matrices)


def to_quarters(pieces):
    sectors, count, sector = pieces.shape
    per = sectors // 4
    if per == 1:
        return pieces
    return pieces.reshape(4, per, count, sector).transpose(0, 2, 1, 3).reshape(4, count, per * sector)


def to_sectors(quarters, sectors):
    _, count, quarter = quarters.shape
    per = sectors // 4
    if per == 1:
        return quarters
    sector = quarter // per
    return quarters.reshape(4, count, per, sector).transpose(0, 2, 1, 3).reshape(sectors, count, sector)


def still_tables(length):
    quarter = length // 4
    target = np.arange(quarter)
    rows = []
    for count in class_counts(length):
        angle = (count * target % (2 * quarter)) * (np.pi / quarter)
        rows += [np.sin(angle), np.cos(angle)]
    angle = target * (2.0 * np.pi / length)
    rows += [np.cos(angle), np.sin(angle)] * 2
    return jnp.asarray(np.stack(rows), jnp.float32)


def turn_values(shift_value, length):
    quarter = length // 4
    even, half = class_counts(length)
    steps = jnp.array([2 * even, 2 * half, 1], jnp.int32) * shift_value
    angle = jnp.remainder(steps, length).astype(jnp.float32) * (2.0 * math.pi / length)
    return jnp.concatenate([jnp.sin(angle), jnp.cos(angle)])


def forward_body(length, block, cells, turn_ref, shift_ref, rows_ref, cols_ref, cycle_ref, out_ref, ghost_ref,
                 land, done, local, mean, ghosts, eh, el, hh, hl, tab, send_sem, recv_sem, mean_send, mean_recv, local_sem, store_sem):
    count = land.shape[1]
    chunks = count // block
    quarter = length // 4
    me = lax.axis_index("az")
    matrices = (eh, el, hh, hl)

    barrier = pltpu.get_barrier_semaphore()
    for k in (1, 2, 3):
        pl.semaphore_signal(barrier, inc=1, device_id={"az": lax.rem(me + k, 4)}, device_id_type=pl.DeviceIdType.MESH)
    pl.semaphore_wait(barrier, 3)

    def part(c):
        return pl.ds(pl.multiple_of(c * block, block), block)

    def send(c, k):
        peer = lax.rem(me + k, 4)
        return pltpu.make_async_remote_copy(
            src_ref=cycle_ref.at[peer, part(c)],
            dst_ref=land.at[me, part(c)],
            send_sem=send_sem.at[c, k - 1],
            recv_sem=recv_sem.at[c, k - 1],
            device_id={"az": peer},
            device_id_type=pl.DeviceIdType.MESH,
        )

    def send_mean(k):
        return pltpu.make_async_remote_copy(
            src_ref=mean.at[me],
            dst_ref=mean.at[me],
            send_sem=mean_send.at[k - 1],
            recv_sem=mean_recv.at[k - 1],
            device_id={"az": lax.rem(me + k, 4)},
            device_id_type=pl.DeviceIdType.MESH,
        )

    def store(c):
        return pltpu.make_async_copy(done.at[:, part(c)], out_ref.at[:, part(c)], store_sem.at[c])

    whole = pltpu.make_async_copy(cycle_ref, local, local_sem.at[0])
    own = pltpu.make_async_copy(cycle_ref.at[me], land.at[me], local_sem.at[1])
    for k in (2, 1, 3):
        send(0, k).start()
    whole.start()
    own.start()

    whole.wait()

    def average(c, carry):
        rows = pl.ds(pl.multiple_of(c * 8 * KR, 8 * KR), 8 * KR)
        total = LAYER_WEIGHTS[0] * local[0, rows]
        for layer in (1, 2, 3):
            total = total + LAYER_WEIGHTS[layer] * local[layer, rows]
        mean[me, pl.ds(pl.multiple_of(c * 8, 8), 8)] = jnp.sum(total.reshape(8, KR, quarter), axis=1) / KR
        return carry

    lax.fori_loop(0, cells // 8, average, 0)
    for k in (2, 1, 3):
        send_mean(k).start()
    for k in (2, 1, 3):
        send(1, k).start()

    tab[...] = rows_ref[...]
    for at, turn in ((0, 0), (2, 1)):
        sine, cosine = rows_ref[at : at + 1, :], rows_ref[at + 1 : at + 2, :]
        tab[at : at + 1, :] = sine * turn_ref[3 + turn] - cosine * turn_ref[turn]
        tab[at + 1 : at + 2, :] = cosine * turn_ref[3 + turn] + sine * turn_ref[turn]
    cosine, sine = rows_ref[4:5, :], rows_ref[5:6, :]
    tab[4:5, :] = cosine * turn_ref[5] + sine * turn_ref[2]
    tab[5:6, :] = sine * turn_ref[5] - cosine * turn_ref[2]

    def build(i, carry):
        first = pl.multiple_of(i * 128, 128)
        rows = pl.ds(first, 128)
        values = matrix_values(length, first, 128, shift_ref[0], tab[...], cols_ref[rows, :])
        for ref, value in zip(matrices, values):
            ref[rows, :] = value
        return carry

    lax.fori_loop(0, quarter // 128, build, 0)
    own.wait()

    def step(c, carry):
        @pl.when(c == chunks - 1)
        def _():
            for k in (1, 2, 3):
                send_mean(k).wait_recv()
            for i, value in enumerate(filter_quarters([mean[i] for i in range(4)], tab, matrices)):
                ghosts[i] = value
            ghost_ref[...] = ghosts[me]

        for k in (2, 1, 3):
            send(c, k).wait_recv()

        @pl.when(c + 2 < chunks)
        def _():
            for k in (2, 1, 3):
                send(c + 2, k).start()

        values = filter_quarters([land[i, part(c)] for i in range(4)], tab, matrices)
        for i, value in enumerate(values):
            done[i, part(c)] = value
        store(c).start()
        return carry

    lax.fori_loop(0, chunks, step, 0)

    def finish(c, carry):
        for k in (1, 2, 3):
            send(c, k).wait_send()
        store(c).wait()
        return carry

    lax.fori_loop(0, chunks, finish, 0)
    for k in (1, 2, 3):
        send_mean(k).wait_send()


def forward(rows, shift, cells):
    sectors, count, sector = rows.shape
    length = sectors * sector
    block = 64
    chunks = count // block
    f32, bf16 = jnp.float32, jnp.bfloat16
    smem = pl.BlockSpec(memory_space=pltpu.SMEM)
    vmem = pl.BlockSpec(memory_space=pltpu.VMEM)
    hbm = pl.BlockSpec(memory_space=pl.ANY)
    dma = pltpu.SemaphoreType.DMA
    return pl.pallas_call(
        lambda *refs: forward_body(length, block, cells, *refs),
        out_shape=[jax.ShapeDtypeStruct(rows.shape, f32), jax.ShapeDtypeStruct((cells, sector), f32)],
        in_specs=[smem, smem, vmem, vmem, hbm],
        out_specs=[hbm, vmem],
        scratch_shapes=[pltpu.VMEM(rows.shape, f32)] * 3
        + [pltpu.VMEM((4, cells, sector), f32)] * 2
        + [pltpu.VMEM((sector, sector), bf16)] * 4
        + [pltpu.VMEM((8, sector), f32), dma((chunks, 3)), dma((chunks, 3)), dma((3,)), dma((3,)), dma((2,)), dma((chunks,))],
        compiler_params=pltpu.CompilerParams(vmem_limit_bytes=52 * MIB, collective_id=0, has_side_effects=True),
        cost_estimate=pl.CostEstimate(flops=24 * count * sector * sector, bytes_accessed=12 * count * length, transcendentals=0),
        name="forward_filter",
    )(turn_values(shift[0], length), shift, still_tables(length), source_tables(length), rows)


def shifted(array, axis, dim, width):
    devices, length = (lax.axis_size(axis), array.shape[dim])
    up = [(i, (i + 1) % devices) for i in range(devices - 1)]
    down = [(j, i) for i, j in up]
    last = lax.slice_in_dim(array, length - width, length, axis=dim)
    leading = lax.slice_in_dim(array, 0, width, axis=dim)
    return lax.ppermute(last, axis, up), lax.ppermute(leading, axis, down)


def chunked(cycle, shift):
    layers, variables, radial, sector = cycle.shape
    sectors = lax.axis_size("az")
    length = sectors * sector
    shift_value = shift[0]
    tables = shift_tables(shift_value, length)
    matrices = filter_matrices(shift, tables, length)

    def across(part):
        return lax.all_to_all(part, "az", split_axis=0, concat_axis=0, tiled=True)

    def passed(pieces):
        return to_sectors(filtered(to_quarters(pieces), tables, matrices), sectors)

    lead = cycle[:1].reshape(sectors, -1, sector)
    rest = cycle[1:].reshape(sectors, -1, sector)
    lead = across(lead)

    weights = jnp.array(LAYER_WEIGHTS, jnp.float32)
    cells = radial // KR
    grouped = cycle.reshape(layers, variables, cells, KR, sector)
    mean = jnp.sum(jnp.sum(grouped * weights[:, None, None, None, None], axis=0), axis=2) / KR
    around = lax.all_gather(mean.reshape(variables * cells, sector), "az", axis=0, tiled=False)
    lead, around, rest = lax.optimization_barrier((lead, around, rest))
    rest = across(rest)

    ghost = lax.dynamic_index_in_dim(passed(around), lax.axis_index("az"), 0, keepdims=False)

    lead, rest = lax.optimization_barrier((passed(lead), rest))
    lead = across(lead).reshape(1, variables, radial, sector)
    rest = across(passed(rest)).reshape(layers - 1, variables, radial, sector)
    shifted_cycle = jnp.concatenate([lead, rest], axis=0)
    return ghost, shifted_cycle


def on_device(cycle, field, shift, owner):
    layers, variables, radial, sector = cycle.shape
    sectors = lax.axis_size("az")
    cells = variables * (radial // KR)
    if sectors == layers == 4 and variables * radial % 64 == 0 and variables * radial >= 128 and cells % 8 == 0:
        moved, ghost = forward(cycle.reshape(layers, variables * radial, sector), shift, cells)
        shifted_cycle = lax.all_to_all(moved.reshape(cycle.shape), "az", split_axis=0, concat_axis=0, tiled=True)
    else:
        ghost, shifted_cycle = chunked(cycle, shift)
    ghost = lax.all_gather(ghost.reshape(variables, radial // KR, sector), "ax", axis=1, tiled=True)

    mask = owner.astype(jnp.float32)[None, :, :, None]
    speeds = jnp.array(AXIAL_SPEEDS, jnp.float32)[:, None, None, None]
    at_inlet = lax.axis_index("ax") == 0

    def rates(state):
        inner, outer = shifted(state, "rad", 1, 1)
        under, over = shifted(state, "ax", 2, 1)
        lower = jnp.where(at_inlet, ghost[:, :, None], under)
        outward = jnp.concatenate([state[:, 1:], outer], axis=1)
        inward = jnp.concatenate([inner, state[:, :-1]], axis=1)
        above = jnp.concatenate([state[:, :, 1:], over], axis=2)
        below = jnp.concatenate([lower, state[:, :, :-1]], axis=2)
        return mask * (
            DIFFUSION * (outward + inward + above + below - 4.0 * state)
            - 0.5 * speeds * (above - below)
            - 0.5 * SWIRL_SPEED * (outward - inward)
        )

    first = rates(field)
    second = rates(field + 0.5 * first)
    third = rates(field + 0.5 * second)
    fourth = rates(field + third)
    field_next = field + (first + 2.0 * second + 2.0 * third + fourth) / 6.0
    return (field_next, shifted_cycle)


def solution(mesh):
    in_specs = (P(None, None, ("rad", "ax"), "az"), P(None, "rad", "ax", "az"), P(), P("rad", "ax"))
    out_specs = (P(None, "rad", "ax", "az"), P(None, None, ("rad", "ax"), "az"))
    return jax.shard_map(
        on_device, mesh=mesh, in_specs=in_specs, out_specs=out_specs, check_vma=False
    )
```

```python
import math

import jax
import jax.numpy as jnp
import numpy as np
from jax import lax
from jax.experimental import pallas as pl
from jax.experimental.pallas import tpu as pltpu
from jax.sharding import PartitionSpec as P

KR = 8


LAYER_WEIGHTS = (0.4, 0.3, 0.2, 0.1)
AXIAL_SPEEDS = (0.35, 0.2, 0.3, 0.25, 0.4)
DIFFUSION = 0.15
SWIRL_SPEED = 0.1
MIB = 1024 * 1024


def class_counts(length):
    top = (length - 1) // 3
    kept = np.arange(-top, top + 1)
    first = kept[kept % 4 == 1]
    assert length % 4 == 0 and (first - 1).sum() == 0
    even, odd, half = [int((kept % 4 == r).sum()) for r in (0, 1, 2)]
    assert even == odd
    return even, half


def shift_tables(shift_value, length):
    quarter = length // 4
    even, half = class_counts(length)
    target = jnp.arange(quarter, dtype=jnp.int32) - shift_value
    rows = []
    for count in (even, half):
        angle = jnp.remainder(count * target, 2 * quarter).astype(jnp.float32) * (math.pi / quarter)
        rows += [jnp.sin(angle), jnp.cos(angle)]
    angle = jnp.remainder(target, length).astype(jnp.float32) * (2.0 * math.pi / length)
    rows += [jnp.cos(angle), jnp.sin(angle)]
    source = np.arange(quarter) * (2.0 * np.pi / length)
    rows += [jnp.asarray(np.cos(source), jnp.float32), jnp.asarray(np.sin(source), jnp.float32)]
    return jnp.stack(rows)


def source_tables(length):
    quarter = length // 4
    source = np.arange(quarter)
    cols = []
    for count in class_counts(length):
        angle = (count * source % (2 * quarter)) * (np.pi / quarter)
        cols += [np.sin(angle), np.cos(angle)]
    return jnp.asarray(np.stack(cols, axis=1), jnp.float32)


def matrix_values(length, first, block, shift_value, rows, cols):
    quarter = length // 4
    even, half = class_counts(length)
    shape = (block, quarter)
    source = lax.broadcasted_iota(jnp.int32, shape, 0) + first
    target = lax.broadcasted_iota(jnp.int32, shape, 1)
    apart = (target - source - shift_value) & (2 * quarter - 1)
    apart = jnp.where(apart >= quarter, apart - 2 * quarter, apart)
    near = jnp.where(apart > quarter // 2, quarter - apart, apart)
    near = jnp.where(apart < -(quarter // 2), -quarter - apart, near)
    u = near.astype(jnp.float32) * (math.pi / quarter)
    w = u * u
    poly = jnp.full(shape, 1.0 / 6227020800.0, jnp.float32)
    for c in (-1.0 / 39916800.0, 1.0 / 362880.0, -1.0 / 5040.0, 1.0 / 120.0, -1.0 / 6.0):
        poly = poly * w + c
    sine = u + u * (w * poly)
    zero = near == 0
    inverse = 0.25 / (quarter * jnp.where(zero, 1.0, sine))
    top_even = rows[0:1, :] * cols[:, 1:2] - rows[1:2, :] * cols[:, 0:1]
    top_half = rows[2:3, :] * cols[:, 3:4] - rows[3:4, :] * cols[:, 2:3]
    sign = jnp.where(apart == 0, 1.0, -1.0)
    m_even = jnp.where(zero, 0.25 * even / quarter, top_even * inverse)
    m_half = jnp.where(zero, sign * (0.25 * half / quarter), top_half * inverse)
    return split(m_even) + split(m_half)


def kernel_matrix_body(length, block, shift_ref, rows_ref, cols_ref, *out_refs):
    first = pl.program_id(0) * block
    values = matrix_values(length, first, block, shift_ref[0], rows_ref[...], cols_ref[...])
    for ref, value in zip(out_refs, values):
        ref[...] = value


def filter_matrices(shift, tables, length):
    quarter = length // 4
    block = 128
    out = jax.ShapeDtypeStruct((quarter, quarter), jnp.bfloat16)
    return pl.pallas_call(
        lambda *refs: kernel_matrix_body(length, block, *refs),
        grid=(quarter // block,),
        out_shape=[out] * 4,
        in_specs=[
            pl.BlockSpec(memory_space=pltpu.SMEM),
            pl.BlockSpec((8, quarter), lambda i: (0, 0)),
            pl.BlockSpec((block, 4), lambda i: (i, 0)),
        ],
        out_specs=[pl.BlockSpec((block, quarter), lambda i: (i, 0))] * 4,
        compiler_params=pltpu.CompilerParams(vmem_limit_bytes=32 * MIB),
        cost_estimate=pl.CostEstimate(flops=60 * quarter * quarter, bytes_accessed=8 * quarter * quarter, transcendentals=0),
        name="filter_matrices",
    )(shift, tables, source_tables(length))


def split(value):
    high = value.astype(jnp.bfloat16)
    return high, (value - high.astype(jnp.float32)).astype(jnp.bfloat16)


def product(value, high_ref, low_ref):
    high, low = split(value)
    f32 = jnp.float32
    return (
        jnp.dot(high, low_ref[...], preferred_element_type=f32)
        + jnp.dot(low, high_ref[...], preferred_element_type=f32)
        + jnp.dot(high, high_ref[...], preferred_element_type=f32)
    )


def filter_quarters(parts, tab_ref, matrix_refs):
    x0, x1, x2, x3 = parts
    count = x0.shape[0]
    eh_ref, el_ref, hh_ref, hl_ref = matrix_refs
    cos_t, sin_t = 2.0 * tab_ref[4:5, :], 2.0 * tab_ref[5:6, :]
    cos_s, sin_s = tab_ref[6:7, :], tab_ref[7:8, :]
    even, odd = x0 + x2, x1 + x3
    re, im = x0 - x2, x3 - x1
    stacked = jnp.concatenate([even + odd, re * cos_s + im * sin_s, im * cos_s - re * sin_s], axis=0)
    turned = product(stacked, eh_ref, el_ref)
    z2 = product(even - odd, hh_ref, hl_ref)
    z0, ure, uim = turned[:count], turned[count : 2 * count], turned[2 * count :]
    zre = cos_t * ure - sin_t * uim
    zim = cos_t * uim + sin_t * ure
    plus, minus = z0 + z2, z0 - z2
    return plus + zre, minus - zim, plus - zre, minus + zim


def filter_body(x_ref, tab_ref, eh_ref, el_ref, hh_ref, hl_ref, out_ref):
    values = filter_quarters([x_ref[i] for i in range(4)], tab_ref, (eh_ref, el_ref, hh_ref, hl_ref))
    for i, value in enumerate(values):
        out_ref[i] = value


def filtered(quarters, tables, matrices):
    _, count, quarter = quarters.shape
    block = next((b for b in (80, 64, 40, 32, 16, 8) if count % b == 0), count)
    whole = pl.BlockSpec((quarter, quarter), lambda i: (0, 0))
    part = pl.BlockSpec((4, block, quarter), lambda i: (0, i, 0))
    return pl.pallas_call(
        filter_body,
        grid=(count // block,),
        out_shape=jax.ShapeDtypeStruct(quarters.shape, jnp.float32),
        in_specs=[part, pl.BlockSpec((8, quarter), lambda i: (0, 0))] + [whole] * 4,
        out_specs=part,
        compiler_params=pltpu.CompilerParams(vmem_limit_bytes=48 * MIB),
        cost_estimate=pl.CostEstimate(
            flops=24 * count * quarter * quarter,
            bytes_accessed=32 * count * quarter + 8 * quarter * quarter,
            transcendentals=0,
        ),
        name="spectral_filter",
    )(quarters, tables, *matrices)


def to_quarters(pieces):
    sectors, count, sector = pieces.shape
    per = sectors // 4
    if per == 1:
        return pieces
    return pieces.reshape(4, per, count, sector).transpose(0, 2, 1, 3).reshape(4, count, per * sector)


def to_sectors(quarters, sectors):
    _, count, quarter = quarters.shape
    per = sectors // 4
    if per == 1:
        return quarters
    sector = quarter // per
    return quarters.reshape(4, count, per, sector).transpose(0, 2, 1, 3).reshape(sectors, count, sector)


def still_tables(length):
    quarter = length // 4
    target = np.arange(quarter)
    rows = []
    for count in class_counts(length):
        angle = (count * target % (2 * quarter)) * (np.pi / quarter)
        rows += [np.sin(angle), np.cos(angle)]
    angle = target * (2.0 * np.pi / length)
    rows += [np.cos(angle), np.sin(angle)] * 2
    return jnp.asarray(np.stack(rows), jnp.float32)


def turn_values(shift_value, length):
    quarter = length // 4
    even, half = class_counts(length)
    steps = jnp.array([2 * even, 2 * half, 1], jnp.int32) * shift_value
    angle = jnp.remainder(steps, length).astype(jnp.float32) * (2.0 * math.pi / length)
    return jnp.concatenate([jnp.sin(angle), jnp.cos(angle)])


def forward_body(length, block, cells, turn_ref, shift_ref, rows_ref, cols_ref, cycle_ref, out_ref, ghost_ref,
                 land, done, local, mean, ghosts, eh, el, hh, hl, tab, send_sem, recv_sem, mean_send, mean_recv, local_sem, store_sem):
    count = land.shape[1]
    chunks = count // block
    quarter = length // 4
    me = lax.axis_index("az")
    matrices = (eh, el, hh, hl)

    barrier = pltpu.get_barrier_semaphore()
    for k in (1, 2, 3):
        pl.semaphore_signal(barrier, inc=1, device_id={"az": lax.rem(me + k, 4)}, device_id_type=pl.DeviceIdType.MESH)
    pl.semaphore_wait(barrier, 3)

    def part(c):
        return pl.ds(pl.multiple_of(c * block, block), block)

    def send(c, k):
        peer = lax.rem(me + k, 4)
        return pltpu.make_async_remote_copy(
            src_ref=cycle_ref.at[peer, part(c)],
            dst_ref=land.at[me, part(c)],
            send_sem=send_sem.at[c, k - 1],
            recv_sem=recv_sem.at[c, k - 1],
            device_id={"az": peer},
            device_id_type=pl.DeviceIdType.MESH,
        )

    def send_mean(k):
        return pltpu.make_async_remote_copy(
            src_ref=mean.at[me],
            dst_ref=mean.at[me],
            send_sem=mean_send.at[k - 1],
            recv_sem=mean_recv.at[k - 1],
            device_id={"az": lax.rem(me + k, 4)},
            device_id_type=pl.DeviceIdType.MESH,
        )

    def store(c):
        return pltpu.make_async_copy(done.at[:, part(c)], out_ref.at[:, part(c)], store_sem.at[c])

    whole = pltpu.make_async_copy(cycle_ref, local, local_sem.at[0])
    own = pltpu.make_async_copy(cycle_ref.at[me], land.at[me], local_sem.at[1])
    for k in (2, 1, 3):
        send(0, k).start()
    whole.start()
    own.start()

    whole.wait()

    def average(c, carry):
        rows = pl.ds(pl.multiple_of(c * 8 * KR, 8 * KR), 8 * KR)
        total = LAYER_WEIGHTS[0] * local[0, rows]
        for layer in (1, 2, 3):
            total = total + LAYER_WEIGHTS[layer] * local[layer, rows]
        mean[me, pl.ds(pl.multiple_of(c * 8, 8), 8)] = jnp.sum(total.reshape(8, KR, quarter), axis=1) / KR
        return carry

    lax.fori_loop(0, cells // 8, average, 0)
    for k in (2, 1, 3):
        send_mean(k).start()
    for k in (2, 1, 3):
        send(1, k).start()

    tab[...] = rows_ref[...]
    for at, turn in ((0, 0), (2, 1)):
        sine, cosine = rows_ref[at : at + 1, :], rows_ref[at + 1 : at + 2, :]
        tab[at : at + 1, :] = sine * turn_ref[3 + turn] - cosine * turn_ref[turn]
        tab[at + 1 : at + 2, :] = cosine * turn_ref[3 + turn] + sine * turn_ref[turn]
    cosine, sine = rows_ref[4:5, :], rows_ref[5:6, :]
    tab[4:5, :] = cosine * turn_ref[5] + sine * turn_ref[2]
    tab[5:6, :] = sine * turn_ref[5] - cosine * turn_ref[2]

    def build(i, carry):
        first = pl.multiple_of(i * 128, 128)
        rows = pl.ds(first, 128)
        values = matrix_values(length, first, 128, shift_ref[0], tab[...], cols_ref[rows, :])
        for ref, value in zip(matrices, values):
            ref[rows, :] = value
        return carry

    lax.fori_loop(0, quarter // 128, build, 0)
    own.wait()
    for k in (2, 1, 3):
        send(2, k).start()

    def step(c, carry):
        @pl.when(c == chunks - 1)
        def _():
            for k in (1, 2, 3):
                send_mean(k).wait_recv()
            for i, value in enumerate(filter_quarters([mean[i] for i in range(4)], tab, matrices)):
                ghosts[i] = value
            ghost_ref[...] = ghosts[me]

        for k in (2, 1, 3):
            send(c, k).wait_recv()

        @pl.when(c + 3 < chunks)
        def _():
            for k in (2, 1, 3):
                send(c + 3, k).start()

        values = filter_quarters([land[i, part(c)] for i in range(4)], tab, matrices)
        for i, value in enumerate(values):
            done[i, part(c)] = value
        store(c).start()
        return carry

    lax.fori_loop(0, chunks, step, 0)

    def finish(c, carry):
        for k in (1, 2, 3):
            send(c, k).wait_send()
        store(c).wait()
        return carry

    lax.fori_loop(0, chunks, finish, 0)
    for k in (1, 2, 3):
        send_mean(k).wait_send()


def forward(rows, shift, cells):
    sectors, count, sector = rows.shape
    length = sectors * sector
    block = 64
    chunks = count // block
    f32, bf16 = jnp.float32, jnp.bfloat16
    smem = pl.BlockSpec(memory_space=pltpu.SMEM)
    vmem = pl.BlockSpec(memory_space=pltpu.VMEM)
    hbm = pl.BlockSpec(memory_space=pl.ANY)
    dma = pltpu.SemaphoreType.DMA
    return pl.pallas_call(
        lambda *refs: forward_body(length, block, cells, *refs),
        out_shape=[jax.ShapeDtypeStruct(rows.shape, f32), jax.ShapeDtypeStruct((cells, sector), f32)],
        in_specs=[smem, smem, vmem, vmem, hbm],
        out_specs=[hbm, vmem],
        scratch_shapes=[pltpu.VMEM(rows.shape, f32)] * 3
        + [pltpu.VMEM((4, cells, sector), f32)] * 2
        + [pltpu.VMEM((sector, sector), bf16)] * 4
        + [pltpu.VMEM((8, sector), f32), dma((chunks, 3)), dma((chunks, 3)), dma((3,)), dma((3,)), dma((2,)), dma((chunks,))],
        compiler_params=pltpu.CompilerParams(vmem_limit_bytes=52 * MIB, collective_id=0, has_side_effects=True),
        cost_estimate=pl.CostEstimate(flops=24 * count * sector * sector, bytes_accessed=12 * count * length, transcendentals=0),
        name="forward_filter",
    )(turn_values(shift[0], length), shift, still_tables(length), source_tables(length), rows)


def shifted(array, axis, dim, width):
    devices, length = (lax.axis_size(axis), array.shape[dim])
    up = [(i, (i + 1) % devices) for i in range(devices - 1)]
    down = [(j, i) for i, j in up]
    last = lax.slice_in_dim(array, length - width, length, axis=dim)
    leading = lax.slice_in_dim(array, 0, width, axis=dim)
    return lax.ppermute(last, axis, up), lax.ppermute(leading, axis, down)


def chunked(cycle, shift):
    layers, variables, radial, sector = cycle.shape
    sectors = lax.axis_size("az")
    length = sectors * sector
    shift_value = shift[0]
    tables = shift_tables(shift_value, length)
    matrices = filter_matrices(shift, tables, length)

    def across(part):
        return lax.all_to_all(part, "az", split_axis=0, concat_axis=0, tiled=True)

    def passed(pieces):
        return to_sectors(filtered(to_quarters(pieces), tables, matrices), sectors)

    lead = cycle[:1].reshape(sectors, -1, sector)
    rest = cycle[1:].reshape(sectors, -1, sector)
    lead = across(lead)

    weights = jnp.array(LAYER_WEIGHTS, jnp.float32)
    cells = radial // KR
    grouped = cycle.reshape(layers, variables, cells, KR, sector)
    mean = jnp.sum(jnp.sum(grouped * weights[:, None, None, None, None], axis=0), axis=2) / KR
    around = lax.all_gather(mean.reshape(variables * cells, sector), "az", axis=0, tiled=False)
    lead, around, rest = lax.optimization_barrier((lead, around, rest))
    rest = across(rest)

    ghost = lax.dynamic_index_in_dim(passed(around), lax.axis_index("az"), 0, keepdims=False)

    lead, rest = lax.optimization_barrier((passed(lead), rest))
    lead = across(lead).reshape(1, variables, radial, sector)
    rest = across(passed(rest)).reshape(layers - 1, variables, radial, sector)
    shifted_cycle = jnp.concatenate([lead, rest], axis=0)
    return ghost, shifted_cycle


def on_device(cycle, field, shift, owner):
    layers, variables, radial, sector = cycle.shape
    sectors = lax.axis_size("az")
    cells = variables * (radial // KR)
    if sectors == layers == 4 and variables * radial % 64 == 0 and variables * radial >= 192 and cells % 8 == 0:
        moved, ghost = forward(cycle.reshape(layers, variables * radial, sector), shift, cells)
        shifted_cycle = lax.all_to_all(moved.reshape(cycle.shape), "az", split_axis=0, concat_axis=0, tiled=True)
    else:
        ghost, shifted_cycle = chunked(cycle, shift)
    ghost = lax.all_gather(ghost.reshape(variables, radial // KR, sector), "ax", axis=1, tiled=True)

    mask = owner.astype(jnp.float32)[None, :, :, None]
    speeds = jnp.array(AXIAL_SPEEDS, jnp.float32)[:, None, None, None]
    at_inlet = lax.axis_index("ax") == 0

    def rates(state):
        inner, outer = shifted(state, "rad", 1, 1)
        under, over = shifted(state, "ax", 2, 1)
        lower = jnp.where(at_inlet, ghost[:, :, None], under)
        outward = jnp.concatenate([state[:, 1:], outer], axis=1)
        inward = jnp.concatenate([inner, state[:, :-1]], axis=1)
        above = jnp.concatenate([state[:, :, 1:], over], axis=2)
        below = jnp.concatenate([lower, state[:, :, :-1]], axis=2)
        return mask * (
            DIFFUSION * (outward + inward + above + below - 4.0 * state)
            - 0.5 * speeds * (above - below)
            - 0.5 * SWIRL_SPEED * (outward - inward)
        )

    first = rates(field)
    second = rates(field + 0.5 * first)
    third = rates(field + 0.5 * second)
    fourth = rates(field + third)
    field_next = field + (first + 2.0 * second + 2.0 * third + fourth) / 6.0
    return (field_next, shifted_cycle)


def solution(mesh):
    in_specs = (P(None, None, ("rad", "ax"), "az"), P(None, "rad", "ax", "az"), P(), P("rad", "ax"))
    out_specs = (P(None, "rad", "ax", "az"), P(None, None, ("rad", "ax"), "az"))
    return jax.shard_map(
        on_device, mesh=mesh, in_specs=in_specs, out_specs=out_specs, check_vma=False
    )
```

```python
import math

import jax
import jax.numpy as jnp
import numpy as np
from jax import lax
from jax.experimental import pallas as pl
from jax.experimental.pallas import tpu as pltpu
from jax.sharding import PartitionSpec as P

KR = 8


LAYER_WEIGHTS = (0.4, 0.3, 0.2, 0.1)
AXIAL_SPEEDS = (0.35, 0.2, 0.3, 0.25, 0.4)
DIFFUSION = 0.15
SWIRL_SPEED = 0.1
MIB = 1024 * 1024


def class_counts(length):
    top = (length - 1) // 3
    kept = np.arange(-top, top + 1)
    first = kept[kept % 4 == 1]
    assert length % 4 == 0 and (first - 1).sum() == 0
    even, odd, half = [int((kept % 4 == r).sum()) for r in (0, 1, 2)]
    assert even == odd
    return even, half


def shift_tables(shift_value, length):
    quarter = length // 4
    even, half = class_counts(length)
    target = jnp.arange(quarter, dtype=jnp.int32) - shift_value
    rows = []
    for count in (even, half):
        angle = jnp.remainder(count * target, 2 * quarter).astype(jnp.float32) * (math.pi / quarter)
        rows += [jnp.sin(angle), jnp.cos(angle)]
    angle = jnp.remainder(target, length).astype(jnp.float32) * (2.0 * math.pi / length)
    rows += [jnp.cos(angle), jnp.sin(angle)]
    source = np.arange(quarter) * (2.0 * np.pi / length)
    rows += [jnp.asarray(np.cos(source), jnp.float32), jnp.asarray(np.sin(source), jnp.float32)]
    return jnp.stack(rows)


def source_tables(length):
    quarter = length // 4
    source = np.arange(quarter)
    cols = []
    for count in class_counts(length):
        angle = (count * source % (2 * quarter)) * (np.pi / quarter)
        cols += [np.sin(angle), np.cos(angle)]
    return jnp.asarray(np.stack(cols, axis=1), jnp.float32)


def matrix_values(length, first, block, shift_value, rows, cols):
    quarter = length // 4
    even, half = class_counts(length)
    shape = (block, quarter)
    source = lax.broadcasted_iota(jnp.int32, shape, 0) + first
    target = lax.broadcasted_iota(jnp.int32, shape, 1)
    apart = (target - source - shift_value) & (2 * quarter - 1)
    apart = jnp.where(apart >= quarter, apart - 2 * quarter, apart)
    near = jnp.where(apart > quarter // 2, quarter - apart, apart)
    near = jnp.where(apart < -(quarter // 2), -quarter - apart, near)
    u = near.astype(jnp.float32) * (math.pi / quarter)
    w = u * u
    poly = jnp.full(shape, 1.0 / 6227020800.0, jnp.float32)
    for c in (-1.0 / 39916800.0, 1.0 / 362880.0, -1.0 / 5040.0, 1.0 / 120.0, -1.0 / 6.0):
        poly = poly * w + c
    sine = u + u * (w * poly)
    zero = near == 0
    inverse = 0.25 / (quarter * jnp.where(zero, 1.0, sine))
    top_even = rows[0:1, :] * cols[:, 1:2] - rows[1:2, :] * cols[:, 0:1]
    top_half = rows[2:3, :] * cols[:, 3:4] - rows[3:4, :] * cols[:, 2:3]
    sign = jnp.where(apart == 0, 1.0, -1.0)
    m_even = jnp.where(zero, 0.25 * even / quarter, top_even * inverse)
    m_half = jnp.where(zero, sign * (0.25 * half / quarter), top_half * inverse)
    return split(m_even) + split(m_half)


def kernel_matrix_body(length, block, shift_ref, rows_ref, cols_ref, *out_refs):
    first = pl.program_id(0) * block
    values = matrix_values(length, first, block, shift_ref[0], rows_ref[...], cols_ref[...])
    for ref, value in zip(out_refs, values):
        ref[...] = value


def filter_matrices(shift, tables, length):
    quarter = length // 4
    block = 128
    out = jax.ShapeDtypeStruct((quarter, quarter), jnp.bfloat16)
    return pl.pallas_call(
        lambda *refs: kernel_matrix_body(length, block, *refs),
        grid=(quarter // block,),
        out_shape=[out] * 4,
        in_specs=[
            pl.BlockSpec(memory_space=pltpu.SMEM),
            pl.BlockSpec((8, quarter), lambda i: (0, 0)),
            pl.BlockSpec((block, 4), lambda i: (i, 0)),
        ],
        out_specs=[pl.BlockSpec((block, quarter), lambda i: (i, 0))] * 4,
        compiler_params=pltpu.CompilerParams(vmem_limit_bytes=32 * MIB),
        cost_estimate=pl.CostEstimate(flops=60 * quarter * quarter, bytes_accessed=8 * quarter * quarter, transcendentals=0),
        name="filter_matrices",
    )(shift, tables, source_tables(length))


def split(value):
    high = value.astype(jnp.bfloat16)
    return high, (value - high.astype(jnp.float32)).astype(jnp.bfloat16)


def product(value, high_ref, low_ref):
    high, low = split(value)
    f32 = jnp.float32
    return (
        jnp.dot(high, low_ref[...], preferred_element_type=f32)
        + jnp.dot(low, high_ref[...], preferred_element_type=f32)
        + jnp.dot(high, high_ref[...], preferred_element_type=f32)
    )


def filter_quarters(parts, tab_ref, matrix_refs):
    x0, x1, x2, x3 = parts
    count = x0.shape[0]
    eh_ref, el_ref, hh_ref, hl_ref = matrix_refs
    cos_t, sin_t = 2.0 * tab_ref[4:5, :], 2.0 * tab_ref[5:6, :]
    cos_s, sin_s = tab_ref[6:7, :], tab_ref[7:8, :]
    even, odd = x0 + x2, x1 + x3
    re, im = x0 - x2, x3 - x1
    stacked = jnp.concatenate([even + odd, re * cos_s + im * sin_s, im * cos_s - re * sin_s], axis=0)
    turned = product(stacked, eh_ref, el_ref)
    z2 = product(even - odd, hh_ref, hl_ref)
    z0, ure, uim = turned[:count], turned[count : 2 * count], turned[2 * count :]
    zre = cos_t * ure - sin_t * uim
    zim = cos_t * uim + sin_t * ure
    plus, minus = z0 + z2, z0 - z2
    return plus + zre, minus - zim, plus - zre, minus + zim


def filter_body(x_ref, tab_ref, eh_ref, el_ref, hh_ref, hl_ref, out_ref):
    values = filter_quarters([x_ref[i] for i in range(4)], tab_ref, (eh_ref, el_ref, hh_ref, hl_ref))
    for i, value in enumerate(values):
        out_ref[i] = value


def filtered(quarters, tables, matrices):
    _, count, quarter = quarters.shape
    block = next((b for b in (80, 64, 40, 32, 16, 8) if count % b == 0), count)
    whole = pl.BlockSpec((quarter, quarter), lambda i: (0, 0))
    part = pl.BlockSpec((4, block, quarter), lambda i: (0, i, 0))
    return pl.pallas_call(
        filter_body,
        grid=(count // block,),
        out_shape=jax.ShapeDtypeStruct(quarters.shape, jnp.float32),
        in_specs=[part, pl.BlockSpec((8, quarter), lambda i: (0, 0))] + [whole] * 4,
        out_specs=part,
        compiler_params=pltpu.CompilerParams(vmem_limit_bytes=48 * MIB),
        cost_estimate=pl.CostEstimate(
            flops=24 * count * quarter * quarter,
            bytes_accessed=32 * count * quarter + 8 * quarter * quarter,
            transcendentals=0,
        ),
        name="spectral_filter",
    )(quarters, tables, *matrices)


def to_quarters(pieces):
    sectors, count, sector = pieces.shape
    per = sectors // 4
    if per == 1:
        return pieces
    return pieces.reshape(4, per, count, sector).transpose(0, 2, 1, 3).reshape(4, count, per * sector)


def to_sectors(quarters, sectors):
    _, count, quarter = quarters.shape
    per = sectors // 4
    if per == 1:
        return quarters
    sector = quarter // per
    return quarters.reshape(4, count, per, sector).transpose(0, 2, 1, 3).reshape(sectors, count, sector)


def still_tables(length):
    quarter = length // 4
    target = np.arange(quarter)
    rows = []
    for count in class_counts(length):
        angle = (count * target % (2 * quarter)) * (np.pi / quarter)
        rows += [np.sin(angle), np.cos(angle)]
    angle = target * (2.0 * np.pi / length)
    rows += [np.cos(angle), np.sin(angle)] * 2
    return jnp.asarray(np.stack(rows), jnp.float32)


def turn_values(shift_value, length):
    quarter = length // 4
    even, half = class_counts(length)
    steps = jnp.array([2 * even, 2 * half, 1], jnp.int32) * shift_value
    angle = jnp.remainder(steps, length).astype(jnp.float32) * (2.0 * math.pi / length)
    return jnp.concatenate([jnp.sin(angle), jnp.cos(angle)])


def forward_body(length, block, cells, turn_ref, shift_ref, rows_ref, cols_ref, cycle_ref, out_ref, ghost_ref,
                 land, done, local, mean, ghosts, eh, el, hh, hl, tab, send_sem, recv_sem, mean_send, mean_recv, local_sem, store_sem):
    count = land.shape[1]
    chunks = count // block
    quarter = length // 4
    me = lax.axis_index("az")
    matrices = (eh, el, hh, hl)

    barrier = pltpu.get_barrier_semaphore()
    for k in (1, 2, 3):
        pl.semaphore_signal(barrier, inc=1, device_id={"az": lax.rem(me + k, 4)}, device_id_type=pl.DeviceIdType.MESH)
    pl.semaphore_wait(barrier, 3)

    def partner(k):
        return (None, me + 1 - 2 * lax.rem(me, 2), lax.rem(me + 2, 4), 3 - me)[k]

    def part(c):
        return pl.ds(pl.multiple_of(c * block, block), block)

    def send(c, k):
        peer = partner(k)
        return pltpu.make_async_remote_copy(
            src_ref=cycle_ref.at[peer, part(c)],
            dst_ref=land.at[me, part(c)],
            send_sem=send_sem.at[c, k - 1],
            recv_sem=recv_sem.at[c, k - 1],
            device_id={"az": peer},
            device_id_type=pl.DeviceIdType.MESH,
        )

    def send_mean(k):
        return pltpu.make_async_remote_copy(
            src_ref=mean.at[me],
            dst_ref=mean.at[me],
            send_sem=mean_send.at[k - 1],
            recv_sem=mean_recv.at[k - 1],
            device_id={"az": partner(k)},
            device_id_type=pl.DeviceIdType.MESH,
        )

    def store(c):
        return pltpu.make_async_copy(done.at[:, part(c)], out_ref.at[:, part(c)], store_sem.at[c])

    whole = pltpu.make_async_copy(cycle_ref, local, local_sem.at[0])
    own = pltpu.make_async_copy(cycle_ref.at[me], land.at[me], local_sem.at[1])
    for k in (2, 3, 1):
        send(0, k).start()
    whole.start()
    own.start()

    whole.wait()

    def average(c, carry):
        rows = pl.ds(pl.multiple_of(c * 8 * KR, 8 * KR), 8 * KR)
        total = LAYER_WEIGHTS[0] * local[0, rows]
        for layer in (1, 2, 3):
            total = total + LAYER_WEIGHTS[layer] * local[layer, rows]
        mean[me, pl.ds(pl.multiple_of(c * 8, 8), 8)] = jnp.sum(total.reshape(8, KR, quarter), axis=1) / KR
        return carry

    lax.fori_loop(0, cells // 8, average, 0)
    for k in (2, 3, 1):
        send_mean(k).start()
    for k in (2, 3, 1):
        send(1, k).start()

    tab[...] = rows_ref[...]
    for at, turn in ((0, 0), (2, 1)):
        sine, cosine = rows_ref[at : at + 1, :], rows_ref[at + 1 : at + 2, :]
        tab[at : at + 1, :] = sine * turn_ref[3 + turn] - cosine * turn_ref[turn]
        tab[at + 1 : at + 2, :] = cosine * turn_ref[3 + turn] + sine * turn_ref[turn]
    cosine, sine = rows_ref[4:5, :], rows_ref[5:6, :]
    tab[4:5, :] = cosine * turn_ref[5] + sine * turn_ref[2]
    tab[5:6, :] = sine * turn_ref[5] - cosine * turn_ref[2]

    def build(i, carry):
        first = pl.multiple_of(i * 128, 128)
        rows = pl.ds(first, 128)
        values = matrix_values(length, first, 128, shift_ref[0], tab[...], cols_ref[rows, :])
        for ref, value in zip(matrices, values):
            ref[rows, :] = value
        return carry

    lax.fori_loop(0, quarter // 128, build, 0)
    own.wait()

    def step(c, carry):
        @pl.when(c == chunks - 1)
        def _():
            for k in (1, 2, 3):
                send_mean(k).wait_recv()
            for i, value in enumerate(filter_quarters([mean[i] for i in range(4)], tab, matrices)):
                ghosts[i] = value
            ghost_ref[...] = ghosts[me]

        for k in (2, 3, 1):
            send(c, k).wait_recv()

        @pl.when(c + 2 < chunks)
        def _():
            for k in (2, 3, 1):
                send(c + 2, k).start()

        values = filter_quarters([land[i, part(c)] for i in range(4)], tab, matrices)
        for i, value in enumerate(values):
            done[i, part(c)] = value
        store(c).start()
        return carry

    lax.fori_loop(0, chunks, step, 0)

    def finish(c, carry):
        for k in (1, 2, 3):
            send(c, k).wait_send()
        store(c).wait()
        return carry

    lax.fori_loop(0, chunks, finish, 0)
    for k in (1, 2, 3):
        send_mean(k).wait_send()


def forward(rows, shift, cells):
    sectors, count, sector = rows.shape
    length = sectors * sector
    block = 64
    chunks = count // block
    f32, bf16 = jnp.float32, jnp.bfloat16
    smem = pl.BlockSpec(memory_space=pltpu.SMEM)
    vmem = pl.BlockSpec(memory_space=pltpu.VMEM)
    hbm = pl.BlockSpec(memory_space=pl.ANY)
    dma = pltpu.SemaphoreType.DMA
    return pl.pallas_call(
        lambda *refs: forward_body(length, block, cells, *refs),
        out_shape=[jax.ShapeDtypeStruct(rows.shape, f32), jax.ShapeDtypeStruct((cells, sector), f32)],
        in_specs=[smem, smem, vmem, vmem, hbm],
        out_specs=[hbm, vmem],
        scratch_shapes=[pltpu.VMEM(rows.shape, f32)] * 3
        + [pltpu.VMEM((4, cells, sector), f32)] * 2
        + [pltpu.VMEM((sector, sector), bf16)] * 4
        + [pltpu.VMEM((8, sector), f32), dma((chunks, 3)), dma((chunks, 3)), dma((3,)), dma((3,)), dma((2,)), dma((chunks,))],
        compiler_params=pltpu.CompilerParams(vmem_limit_bytes=52 * MIB, collective_id=0, has_side_effects=True),
        cost_estimate=pl.CostEstimate(flops=24 * count * sector * sector, bytes_accessed=12 * count * length, transcendentals=0),
        name="forward_filter",
    )(turn_values(shift[0], length), shift, still_tables(length), source_tables(length), rows)


def shifted(array, axis, dim, width):
    devices, length = (lax.axis_size(axis), array.shape[dim])
    up = [(i, (i + 1) % devices) for i in range(devices - 1)]
    down = [(j, i) for i, j in up]
    last = lax.slice_in_dim(array, length - width, length, axis=dim)
    leading = lax.slice_in_dim(array, 0, width, axis=dim)
    return lax.ppermute(last, axis, up), lax.ppermute(leading, axis, down)


def chunked(cycle, shift):
    layers, variables, radial, sector = cycle.shape
    sectors = lax.axis_size("az")
    length = sectors * sector
    shift_value = shift[0]
    tables = shift_tables(shift_value, length)
    matrices = filter_matrices(shift, tables, length)

    def across(part):
        return lax.all_to_all(part, "az", split_axis=0, concat_axis=0, tiled=True)

    def passed(pieces):
        return to_sectors(filtered(to_quarters(pieces), tables, matrices), sectors)

    lead = cycle[:1].reshape(sectors, -1, sector)
    rest = cycle[1:].reshape(sectors, -1, sector)
    lead = across(lead)

    weights = jnp.array(LAYER_WEIGHTS, jnp.float32)
    cells = radial // KR
    grouped = cycle.reshape(layers, variables, cells, KR, sector)
    mean = jnp.sum(jnp.sum(grouped * weights[:, None, None, None, None], axis=0), axis=2) / KR
    around = lax.all_gather(mean.reshape(variables * cells, sector), "az", axis=0, tiled=False)
    lead, around, rest = lax.optimization_barrier((lead, around, rest))
    rest = across(rest)

    ghost = lax.dynamic_index_in_dim(passed(around), lax.axis_index("az"), 0, keepdims=False)

    lead, rest = lax.optimization_barrier((passed(lead), rest))
    lead = across(lead).reshape(1, variables, radial, sector)
    rest = across(passed(rest)).reshape(layers - 1, variables, radial, sector)
    shifted_cycle = jnp.concatenate([lead, rest], axis=0)
    return ghost, shifted_cycle


def on_device(cycle, field, shift, owner):
    layers, variables, radial, sector = cycle.shape
    sectors = lax.axis_size("az")
    cells = variables * (radial // KR)
    if sectors == layers == 4 and variables * radial % 64 == 0 and variables * radial >= 128 and cells % 8 == 0:
        moved, ghost = forward(cycle.reshape(layers, variables * radial, sector), shift, cells)
        shifted_cycle = lax.all_to_all(moved.reshape(cycle.shape), "az", split_axis=0, concat_axis=0, tiled=True)
    else:
        ghost, shifted_cycle = chunked(cycle, shift)
    ghost = lax.all_gather(ghost.reshape(variables, radial // KR, sector), "ax", axis=1, tiled=True)

    mask = owner.astype(jnp.float32)[None, :, :, None]
    speeds = jnp.array(AXIAL_SPEEDS, jnp.float32)[:, None, None, None]
    at_inlet = lax.axis_index("ax") == 0

    def rates(state):
        inner, outer = shifted(state, "rad", 1, 1)
        under, over = shifted(state, "ax", 2, 1)
        lower = jnp.where(at_inlet, ghost[:, :, None], under)
        outward = jnp.concatenate([state[:, 1:], outer], axis=1)
        inward = jnp.concatenate([inner, state[:, :-1]], axis=1)
        above = jnp.concatenate([state[:, :, 1:], over], axis=2)
        below = jnp.concatenate([lower, state[:, :, :-1]], axis=2)
        return mask * (
            DIFFUSION * (outward + inward + above + below - 4.0 * state)
            - 0.5 * speeds * (above - below)
            - 0.5 * SWIRL_SPEED * (outward - inward)
        )

    first = rates(field)
    second = rates(field + 0.5 * first)
    third = rates(field + 0.5 * second)
    fourth = rates(field + third)
    field_next = field + (first + 2.0 * second + 2.0 * third + fourth) / 6.0
    return (field_next, shifted_cycle)


def solution(mesh):
    in_specs = (P(None, None, ("rad", "ax"), "az"), P(None, "rad", "ax", "az"), P(), P("rad", "ax"))
    out_specs = (P(None, "rad", "ax", "az"), P(None, None, ("rad", "ax"), "az"))
    return jax.shard_map(
        on_device, mesh=mesh, in_specs=in_specs, out_specs=out_specs, check_vma=False
    )
```
